32 devices in a mesh: groups: 2 (over x), ctx: 16 (over z, y, core).
Axes of the slice: x: 2, y: 2, z: 4, core: 2. Of those that a mesh axis runs over, the one named last changes fastest.
Arguments:
- queries: bfloat16 [4096, 4096], P(('groups', 'ctx')), parts along dimension 0, may hold values from -130 to 130
- keys_values: bfloat16 [4096, 1024], P(('groups', 'ctx')), parts along dimension 0, may hold values from -25 to 25
- out_grad: bfloat16 [4096, 4096], P(('groups', 'ctx')), parts along dimension 0, may hold values from -6 to 6
- key_blocks: int32 [32, 3], P('groups'), parts along dimension 0, may hold values from 0 to 15, as said below
- key_count: int32 [32], P('groups'), parts along dimension 0, may hold values from 1 to 3, as said below
- block_at_slot: int32 [32], P('groups'), parts along dimension 0, may hold values from 0 to 15, as said below
Outputs:
- attended: bfloat16 [4096, 4096], P(('groups', 'ctx')), parts along dimension 0
- query_grad: bfloat16 [4096, 4096], P(('groups', 'ctx')), parts along dimension 0
- kv_grad: bfloat16 [4096, 1024], P(('groups', 'ctx')), parts along dimension 0
The draws below stay inside these ranges and needn't reach their ends.
There are 2 independent parts, one for each index of `groups`. The reference program is written for one: setup_inputs(seed, part) draws one part's arguments, and reference() takes and returns one part's arrays. A program takes and returns all parts, laid end to end along the dimension named above; each array names one. Nothing has to cross between parts.
Inputs may be any that keep to these rules, and one draw needn't show every extreme that they name: `block_at_slot`: A permutation of the block ids. `key_blocks`: each row lists 3 distinct block ids, the first being the row's own block. Every listed block sits at most 2 slots away from the row's block in the layout of block_at_slot, and some live entry sits exactly 2 slots away. `key_count`: some row has 3 live entries.
All inputs are finite; a program needn't handle non-finite values.
Results may differ from the reference program's by a relative error of at most 0.02.
Values may be sent and summed in bfloat16 or wider, within the bound.
A program may use at most 128 MiB of HBM per device.

```python
import jax
import jax.numpy as jnp
from jax import lax

HEADS = 32
KV_HEADS = 4
HEAD = 128
BLOCK = 128
REACH = 2
KOTH = 2
KMAX = 3
NB = 16
TOKENS = 2048


def mask_tables(key):
    order = jax.random.permutation(jax.random.fold_in(key, 7), NB).astype(jnp.int32)
    slots = jnp.arange(NB, dtype=jnp.int32)
    offsets = jnp.concatenate([jnp.arange(-REACH, 0), jnp.arange(1, REACH + 1)]).astype(jnp.int32)
    targets = slots[:, None] + offsets[None, :]
    inside = (targets >= 0) & (targets < NB)
    raw_scores = jax.random.randint(jax.random.fold_in(key, 8), (NB, 2 * REACH), 0, 1 << 20)
    ranked = raw_scores * (2 * REACH) + jnp.arange(2 * REACH, dtype=jnp.int32)[None, :]
    preferred = jnp.where(slots < NB // 2, REACH, -REACH)
    boosted = (slots[:, None] % 3 == 0) & (offsets[None, :] == preferred[:, None])
    ranked = jnp.where(boosted, ranked + (1 << 26), ranked)
    ranked = jnp.where(inside, ranked, -1)
    unused_top, picked = lax.top_k(ranked, KOTH)
    chosen = jnp.take_along_axis(targets, picked, axis=1)
    slot_lists = jnp.concatenate([slots[:, None], chosen], axis=1).astype(jnp.int32)
    light = jax.random.randint(jax.random.fold_in(key, 9), (NB,), 0, 2)
    heavy = (jax.random.randint(jax.random.fold_in(key, 10), (NB,), 0, 4) == 0).astype(jnp.int32) * (KOTH - 1)
    others = light + heavy
    others = jnp.where(slots % 3 == 0, jnp.maximum(others, 1), others)
    others = jnp.where(slots == 0, KOTH, others)
    table = order[slot_lists]
    block_lists = jnp.zeros((NB, KMAX), jnp.int32).at[order].set(table)
    counts = jnp.zeros((NB,), jnp.int32).at[order].set(1 + others)
    return (block_lists, counts.astype(jnp.int32), order)


def attention_draws(key):
    heads_width = HEADS * HEAD
    pair_width = KV_HEADS * HEAD
    query_part = jnp.clip(jax.random.normal(jax.random.fold_in(key, 21), (TOKENS, heads_width), jnp.float32), -6.0, 6.0)
    key_part = jnp.clip(jax.random.normal(jax.random.fold_in(key, 22), (TOKENS, pair_width), jnp.float32), -6.0, 6.0)
    value_part = jnp.clip(jax.random.normal(jax.random.fold_in(key, 23), (TOKENS, pair_width), jnp.float32), -6.0, 6.0)
    return (query_part, jnp.concatenate([key_part, value_part], axis=1))


def draw_queries(key, part):
    return attention_draws(key)[0].astype(jnp.bfloat16)


def draw_keys_values(key, part):
    return attention_draws(key)[1].astype(jnp.bfloat16)


def draw_key_blocks(key, part):
    return mask_tables(key)[0]


def draw_key_count(key, part):
    return mask_tables(key)[1]


def draw_block_at_slot(key, part):
    return mask_tables(key)[2]


def levels(key, dims, cuts, smallest, top_value):
    def one(position, shards_of):
        steps = jax.random.uniform(jax.random.fold_in(jax.random.fold_in(key, 6), position), (shards_of,), jnp.float32, smallest / len(cuts), top_value / len(cuts))
        return jnp.repeat(jnp.exp(steps), dims[position] // shards_of).reshape((-1,) + (1,) * (len(dims) - position - 1))

    factor_of = one(*cuts[0])
    for cut in cuts[1:]:
        factor_of = factor_of * one(*cut)
    return factor_of


def gaussian(rng, shape, scale, limit, cuts=(), held_as=jnp.bfloat16):
    drawn = scale * jax.random.normal(rng, shape, jnp.float32)
    if cuts:
        drawn = drawn * levels(rng, shape, cuts, -0.22, 0.18)
    return jnp.clip(drawn, -limit, limit).astype(held_as)


def setup_inputs(seed: int = 0, part: int = 0) -> dict:
    arg_keys = jax.random.split(jax.random.key(seed), 7)
    own_keys = jax.random.split(jax.random.fold_in(arg_keys[6], part), 7)
    return {
        "queries": draw_queries(jax.random.fold_in(jax.random.fold_in(arg_keys[6], part), 71), part),
        "keys_values": draw_keys_values(jax.random.fold_in(jax.random.fold_in(arg_keys[6], part), 71), part),
        "out_grad": gaussian(own_keys[2], (TOKENS, HEADS * HEAD), 1.0, 6.0, ((0, 16),)),
        "key_blocks": draw_key_blocks(jax.random.fold_in(jax.random.fold_in(arg_keys[6], part), 71), part),
        "key_count": draw_key_count(jax.random.fold_in(jax.random.fold_in(arg_keys[6], part), 71), part),
        "block_at_slot": draw_block_at_slot(jax.random.fold_in(jax.random.fold_in(arg_keys[6], part), 71), part),
    }


def reference(queries, keys_values, out_grad, key_blocks, key_count, block_at_slot):
    block_count = block_at_slot.shape[0]
    tok_rows = BLOCK
    kv_width = keys_values.shape[1] // 2
    groups = kv_width // HEAD
    repeats = queries.shape[1] // kv_width
    score_scale = HEAD ** -0.5
    slot_range = jnp.arange(block_count, dtype=jnp.int32)
    slot_of_block = jnp.sum(jnp.where(block_at_slot[:, None] == slot_range[None, :], slot_range[:, None], 0), axis=0).astype(jnp.int32)
    row_blocks = key_blocks[block_at_slot]
    key_slots = slot_of_block[row_blocks].astype(jnp.int32)
    live_keys = jnp.arange(KMAX, dtype=jnp.int32)[None, :] < key_count[block_at_slot][:, None]
    query_blocks = queries.reshape(block_count, tok_rows, groups, repeats, HEAD).astype(jnp.float32)
    grad_blocks = out_grad.reshape(block_count, tok_rows, groups, repeats, HEAD).astype(jnp.float32)
    kv_blocks = keys_values.reshape(block_count, tok_rows, 2 * kv_width)

    def per_block(kv_total, inputs):
        query_heads, grad_heads, slots, live = inputs
        chosen = kv_blocks[slots].astype(jnp.float32)
        key_rows = chosen[:, :, :kv_width].reshape(KMAX * tok_rows, groups, HEAD)
        value_rows = chosen[:, :, kv_width:].reshape(KMAX * tok_rows, groups, HEAD)
        bias = jnp.repeat(jnp.where(live, 0.0, -1e30), tok_rows).astype(jnp.float32)
        scores = jnp.einsum("igrd,jgd->grij", query_heads, key_rows) * score_scale + bias
        best_score = jnp.max(scores, axis=-1)
        weights = jnp.exp(scores - best_score[..., None])
        weight_sum = jnp.sum(weights, axis=-1)
        rounded = lax.optimization_barrier(weights.astype(jnp.bfloat16)).astype(jnp.float32)
        mixed = jnp.einsum("grij,jgd->grid", rounded, value_rows) / weight_sum[..., None]
        out_heads = jnp.transpose(mixed, (2, 0, 1, 3)).astype(jnp.bfloat16)
        out_float = lax.optimization_barrier(out_heads).astype(jnp.float32)
        log_total = best_score + jnp.log(weight_sum)
        delta_rows = jnp.einsum("igrd,igrd->gri", grad_heads, out_float)
        probabilities = jnp.exp(scores - log_total[..., None])
        prob_grads = jnp.einsum("igrd,jgd->grij", grad_heads, value_rows)
        score_grads = probabilities * (prob_grads - delta_rows[..., None])
        grads_rounded = lax.optimization_barrier(score_grads.astype(jnp.bfloat16)).astype(jnp.float32)
        probs_rounded = lax.optimization_barrier(probabilities.astype(jnp.bfloat16)).astype(jnp.float32)
        query_term = jnp.einsum("grij,jgd->igrd", grads_rounded, key_rows) * score_scale
        key_term = jnp.einsum("grij,igrd->jgd", grads_rounded, query_heads) * score_scale
        value_term = jnp.einsum("grij,igrd->jgd", probs_rounded, grad_heads)
        kv_term = jnp.concatenate([key_term.reshape(KMAX, tok_rows, kv_width), value_term.reshape(KMAX, tok_rows, kv_width)], axis=2)
        kv_total = kv_total.at[slots].add(kv_term)
        return kv_total, (out_heads.reshape(tok_rows, -1), query_term.reshape(tok_rows, -1).astype(jnp.bfloat16))

    start_total = jnp.zeros((block_count, tok_rows, 2 * kv_width), jnp.float32)
    kv_total, outputs = lax.scan(per_block, start_total, (query_blocks, grad_blocks, key_slots, live_keys))
    attended = outputs[0].reshape(block_count * tok_rows, -1)
    query_grad = outputs[1].reshape(block_count * tok_rows, -1)
    kv_grad = kv_total.reshape(block_count * tok_rows, -1).astype(jnp.bfloat16)
    return (attended, query_grad, kv_grad)
```

```python
import functools

import jax
import jax.numpy as jnp
from jax import lax
from jax.experimental import pallas as pl
from jax.experimental.pallas import tpu as pltpu
from jax.sharding import PartitionSpec as P

HEAD = 128
OFFSETS = (-2, -1, 1, 2)
LOG2E = 1.4426950408889634
NEG = -1e30
NT = (((1,), (1,)), ((), ()))


def kernel(
    n, groups, repeats,
    blocks_ref, count_ref, slot_ref, q_hbm, kv_hbm, do_hbm,
    att, dq, kvg,
    q, kv, do, near, own_grad, gsend, grecv,
    in_sem, kv_sem, near_send, near_recv, grad_send, grad_recv,
):
    rows = q.shape[0]
    wide = repeats * HEAD
    kv_width = groups * HEAD
    scale = HEAD ** (-0.5)
    me = lax.axis_index("ctx")

    def exists(o):
        return jnp.logical_and(me + OFFSETS[o] >= 0, me + OFFSETS[o] < n)

    def exists_at(slot):
        there = me + jnp.where(slot < 2, slot - 2, slot - 1)
        return jnp.logical_and(there >= 0, there < n)

    def target(o):
        return {"ctx": me + OFFSETS[o]}

    def column(g, width):
        return pl.ds(pl.multiple_of(g * width, width), width)

    core = lax.rem(me, 2)
    sibling = {"ctx": me + 1 - 2 * core}
    forward = 3 * (1 - core)
    passed = 1 + core
    beside = 2 - core

    def remote(src, dst, sent, received, device):
        return pltpu.make_async_remote_copy(
            src_ref=src, dst_ref=dst, send_sem=sent, recv_sem=received,
            device_id=device, device_id_type=pl.DeviceIdType.MESH,
        )

    def far_copy(g, o):
        return remote(kv.at[g], near.at[g, 3 - o], near_send.at[g, o], near_recv.at[g, 3 - o], target(o))

    def beside_copy(g):
        return remote(
            kv.at[g], near.at[g, 1 + core], near_send.at[g, 1], near_recv.at[g, 1 + core], sibling
        )

    def relay_copy(g):
        return remote(
            near.at[g, forward], near.at[g, 2 - core], near_send.at[g, 2], near_recv.at[g, 2 - core], sibling
        )

    def near_wait(g, slot):
        remote(
            near.at[g, slot], near.at[g, slot], near_send.at[g, 0], near_recv.at[g, slot], sibling
        ).wait_recv()

    def kv_load(g, part):
        return pltpu.make_async_copy(
            kv_hbm.at[:, pl.ds(part * kv_width + g * HEAD, HEAD)], kv.at[g, part], kv_sem.at[g, part]
        )

    def far_grad(g, o):
        return remote(
            gsend.at[g, o], grecv.at[g, 3 - o], grad_send.at[g, o], grad_recv.at[g, 3 - o], target(o)
        )

    def beside_grad(g):
        return remote(gsend.at[g, beside], grecv.at[g, 1], grad_send.at[g, 1], grad_recv.at[g, 1], sibling)

    def passed_grad(g):
        return remote(gsend.at[g, passed], grecv.at[g, 2], grad_send.at[g, 2], grad_recv.at[g, 2], sibling)

    def relay(g):
        @pl.when(exists_at(forward))
        def _():
            near_wait(g, forward)
            relay_copy(g).start()

    def combine(g):
        @pl.when(exists_at(forward))
        def _():
            passed_grad(g).wait_recv()
            both = gsend[g, forward].astype(jnp.float32) + grecv[g, 2].astype(jnp.float32)
            gsend[g, forward] = both.astype(jnp.bfloat16)

        for o, mine in ((3, 0), (0, 1)):

            @pl.when(jnp.logical_and(exists(o), core == mine))
            def _():
                far_grad(g, o).start()

    def load_copies(g):
        return (
            pltpu.make_async_copy(q_hbm.at[:, column(g, wide)], q.at[:, column(g, wide)], in_sem.at[g, 0]),
            pltpu.make_async_copy(do_hbm.at[:, column(g, wide)], do.at[:, column(g, wide)], in_sem.at[g, 1]),
        )

    for g in range(groups):
        for part in range(2):
            kv_load(g, part).start()
    for copy in load_copies(0):
        copy.start()
    barrier = pltpu.get_barrier_semaphore()
    pl.semaphore_signal(barrier, inc=1, device_id=sibling, device_id_type=pl.DeviceIdType.MESH)
    for o in (0, 3):

        @pl.when(exists(o))
        def _():
            pl.semaphore_signal(barrier, inc=1, device_id=target(o), device_id_type=pl.DeviceIdType.MESH)

    for o in range(4):

        @pl.when(jnp.logical_not(exists(o)))
        def _():
            near[:, o] = jnp.zeros((groups, 2, rows, HEAD), near.dtype)
            if o in (0, 3):
                grecv[:, o] = jnp.zeros((groups, 2, rows, HEAD), grecv.dtype)

    pl.semaphore_wait(barrier, 1 + exists(0).astype(jnp.int32) + exists(3).astype(jnp.int32))

    for g in range(groups):
        kv_load(g, 0).wait()
        kv_load(g, 1).wait()
        for o in (3, 0):

            @pl.when(exists(o))
            def _():
                far_copy(g, o).start()

        beside_copy(g).start()
        if g > 0:
            for copy in load_copies(g):
                copy.start()

    own_block = slot_ref[me]
    live_count = count_ref[own_block]
    chosen = []
    bias = []
    for j in (1, 2):
        wanted = blocks_ref[j, own_block]
        hits = []
        for o in range(4):
            there = jnp.clip(me + OFFSETS[o], 0, n - 1)
            hits.append(exists(o) & (slot_ref[there] == wanted) & (live_count > j))
        chosen.append(hits)
        bias.append(jnp.where(hits[0] | hits[1] | hits[2] | hits[3], 0.0, NEG).astype(jnp.float32))

    def pick(g, part, hits):
        value = near[g, 0, part]
        for o in range(1, 4):
            value = jnp.where(hits[o], near[g, o, part], value)
        return value

    def step(g, carry):
        for copy in load_copies(g):
            copy.wait()
        near_wait(g, beside)

        @pl.when(exists_at(3 - forward))
        def _():
            near_wait(g, 3 - forward)

        @pl.when(exists_at(passed))
        def _():
            near_wait(g, passed)

        @pl.when(g > 0)
        def _():
            combine(g - 1)

        own_key = kv[g, 0]
        own_value = kv[g, 1]
        keys = jnp.concatenate([own_key, pick(g, 0, chosen[0]), pick(g, 0, chosen[1])], axis=0)
        values = jnp.concatenate([own_value, pick(g, 1, chosen[0]), pick(g, 1, chosen[1])], axis=0)
        keys_t = keys.T
        values_t = values.T
        key_grad = jnp.zeros((3 * rows, HEAD), jnp.float32)
        value_grad = jnp.zeros((3 * rows, HEAD), jnp.float32)
        for pair in range(repeats // 2):
            starts = [pl.multiple_of(g * wide + (2 * pair + i) * HEAD, HEAD) for i in range(2)]
            q2 = jnp.concatenate([q[:, pl.ds(s, HEAD)] for s in starts], axis=0)
            do2 = jnp.concatenate([do[:, pl.ds(s, HEAD)] for s in starts], axis=0)
            raw = lax.dot_general(keys, q2, NT, preferred_element_type=jnp.float32) * (scale * LOG2E)
            scores = jnp.concatenate(
                [raw[:rows], raw[rows : 2 * rows] + bias[0], raw[2 * rows :] + bias[1]], axis=0
            )
            best = jnp.max(scores, axis=0, keepdims=True)
            weights = jnp.exp2(scores - best)
            total = jnp.sum(weights, axis=0, keepdims=True)
            probs = weights * (1.0 / total)
            rounded = probs.astype(jnp.bfloat16)
            prob_grads = lax.dot_general(values, do2, NT, preferred_element_type=jnp.float32)
            delta = jnp.sum(probs * prob_grads, axis=0, keepdims=True)
            score_grads = (probs * (prob_grads - delta)).astype(jnp.bfloat16)
            mixed = jnp.dot(values_t, rounded, preferred_element_type=jnp.float32)
            query_grad = jnp.dot(keys_t, score_grads, preferred_element_type=jnp.float32) * scale
            mixed = mixed.astype(jnp.bfloat16).T
            query_grad = query_grad.astype(jnp.bfloat16).T
            for i in range(2):
                att[:, pl.ds(starts[i], HEAD)] = mixed[i * rows : (i + 1) * rows]
                dq[:, pl.ds(starts[i], HEAD)] = query_grad[i * rows : (i + 1) * rows]
            if pair == 1:

                @pl.when(g + 1 < groups)
                def _():
                    relay(g + 1)

            key_grad = key_grad + jnp.dot(score_grads, q2, preferred_element_type=jnp.float32)
            value_grad = value_grad + jnp.dot(rounded, do2, preferred_element_type=jnp.float32)
        for part, grad in ((0, key_grad * scale), (1, value_grad)):
            own_grad[g, part] = grad[:rows]
            for o in range(4):
                gsend[g, o, part] = jnp.where(
                    chosen[0][o], grad[rows : 2 * rows], jnp.where(chosen[1][o], grad[2 * rows :], 0.0)
                ).astype(jnp.bfloat16)
        @pl.when(exists_at(passed))
        def _():
            passed_grad(g).start()

        for o, mine in ((3, 1), (0, 0)):

            @pl.when(jnp.logical_and(exists(o), core == mine))
            def _():
                far_grad(g, o).start()

        beside_grad(g).start()
        return carry

    relay(0)
    lax.fori_loop(0, groups, step, 0)
    combine(groups - 1)

    def finish(g, carry):
        for o in (0, 3):

            @pl.when(exists(3 - o))
            def _():
                far_grad(g, o).wait_recv()

        beside_grad(g).wait_recv()

        for part in range(2):
            total = own_grad[g, part]
            for o in (0, 1, 3):
                total = total + grecv[g, o, part].astype(jnp.float32)
            kvg[:, pl.ds(pl.multiple_of(part * kv_width + g * HEAD, HEAD), HEAD)] = total.astype(jnp.bfloat16)
        return carry

    lax.fori_loop(0, groups, finish, 0)

    def drain(g, carry):
        for o in (0, 3):

            @pl.when(exists(o))
            def _():
                far_copy(g, o).wait_send()
                far_grad(g, o).wait_send()

        @pl.when(exists_at(forward))
        def _():
            relay_copy(g).wait_send()

        @pl.when(exists_at(passed))
        def _():
            passed_grad(g).wait_send()

        beside_copy(g).wait_send()
        beside_grad(g).wait_send()
        return carry

    lax.fori_loop(0, groups, drain, 0)


def flush(att, dq, kvg, att_out, dq_out, kvg_out, out_sem):
    width = kvg.shape[1]
    pieces = [(kvg, kvg_out, 0)]
    for start in range(0, att.shape[1], width):
        pieces.append((att, att_out, start))
        pieces.append((dq, dq_out, start))
    stores = []
    for i, (source, result, start) in enumerate(pieces):
        part = pl.ds(start, width)
        stores.append(pltpu.make_async_copy(source.at[:, part], result.at[:, part], out_sem.at[i]))
    for store in stores:
        store.start()
    for store in stores:
        store.wait()


def body(queries, keys_values, out_grad, key_blocks, key_count, block_at_slot):
    n = lax.axis_size("ctx")
    rows, width = queries.shape
    kv_width = keys_values.shape[1] // 2
    groups = kv_width // HEAD
    repeats = width // kv_width
    anywhere = pl.BlockSpec(memory_space=pl.ANY)
    scalars = pl.BlockSpec(memory_space=pltpu.SMEM)
    wide = pltpu.VMEM((rows, width), jnp.bfloat16)
    narrow = pltpu.VMEM((rows, 2 * kv_width), jnp.bfloat16)
    ring = pltpu.VMEM((groups, 4, 2, rows, HEAD), jnp.bfloat16)
    dma = pltpu.SemaphoreType.DMA
    shapes = (
        jax.ShapeDtypeStruct((rows, width), jnp.bfloat16),
        jax.ShapeDtypeStruct((rows, width), jnp.bfloat16),
        jax.ShapeDtypeStruct((rows, 2 * kv_width), jnp.bfloat16),
    )
    pieces = 2 * (width // (2 * kv_width)) + 1
    held = pl.BlockSpec(memory_space=pltpu.VMEM)
    results = pl.pallas_call(
        functools.partial(kernel, n, groups, repeats),
        out_shape=(wide, wide, narrow),
        in_specs=[scalars] * 3 + [pl.BlockSpec(memory_space=pltpu.HBM)] * 3,
        out_specs=(held, held, held),
        scratch_shapes=[
            wide, pltpu.VMEM((groups, 2, rows, HEAD), jnp.bfloat16), wide,
            ring, pltpu.VMEM((groups, 2, rows, HEAD), jnp.float32), ring, ring,
            dma((groups, 2)), dma((groups, 2)),
            dma((groups, 4)), dma((groups, 4)), dma((groups, 4)), dma((groups, 4)),
        ],
        compiler_params=pltpu.CompilerParams(
            collective_id=0, has_side_effects=True, vmem_limit_bytes=61 * 1024 * 1024
        ),
    )(key_blocks.T, key_count, block_at_slot, queries, keys_values, out_grad)
    return pl.pallas_call(
        flush,
        out_shape=shapes,
        in_specs=[held] * 3,
        out_specs=(pl.BlockSpec(memory_space=pltpu.HBM),) * 3,
        scratch_shapes=[dma((pieces,))],
        compiler_params=pltpu.CompilerParams(vmem_limit_bytes=16 * 1024 * 1024),
    )(*results)


def solution(mesh):
    sharded = P(("groups", "ctx"), None)
    return jax.shard_map(
        body,
        mesh=mesh,
        in_specs=(sharded, sharded, sharded, P("groups", None), P("groups"), P("groups")),
        out_specs=(sharded, sharded, sharded),
        check_vma=False,
    )
```

```python
import functools

import jax
import jax.numpy as jnp
from jax import lax
from jax.experimental import pallas as pl
from jax.experimental.pallas import tpu as pltpu
from jax.sharding import PartitionSpec as P

HEAD = 128
OFFSETS = (-2, -1, 1, 2)
LOG2E = 1.4426950408889634
NEG = -1e30
NT = (((1,), (1,)), ((), ()))
KV_DIRECT = ()
GRAD_DIRECT = ()
COMM = True
EARLY = 4
PEERS = 1
GCOMM = True
CHUNK = 32
DEPTH = 2
COMP = True


class Nop:
    def start(self):
        pass

    def wait_send(self):
        pass

    def wait_recv(self):
        pass


def among(g, members):
    if isinstance(g, int):
        return g in members
    found = jnp.bool_(False)
    for m in members:
        found = jnp.logical_or(found, g == m)
    return found


def kernel(
    n, groups, repeats,
    blocks_ref, count_ref, slot_ref, q_hbm, kv_hbm, do_hbm,
    att, dq, kvg,
    q, kv, do, near, picked, probs, dscores, score, pgrad, own_grad, gsend, grecv,
    in_sem, kv_sem, near_send, near_recv, grad_send, grad_recv,
):
    rows = q.shape[0]
    wide = repeats * HEAD
    kv_width = groups * HEAD
    pairs = repeats // 2
    scale = HEAD ** (-0.5)
    me = lax.axis_index("ctx")
    core = lax.rem(me, 2)
    side = lax.rem(me // 2, 2)
    along = 4 - 8 * side

    def inside(d):
        return jnp.logical_and(me + d >= 0, me + d < n)

    def exists(o):
        return inside(OFFSETS[o])

    sibling = {"ctx": me + 1 - 2 * core}
    partner = {"ctx": me + 2 - 4 * side}
    diagonal = {"ctx": me - 2 + 4 * side}
    ahead = {"ctx": me + along}
    behind = {"ctx": me - along}
    has_ahead = inside(along)
    has_behind = inside(-along)
    partner_slot = 3 - 3 * side
    diag_slot = 3 * side
    forward = 3 * (1 - core)
    free = 3 * core
    passed = 1 + core
    beside = 2 - core
    has_passed = inside(2 * core - 1)
    has_forward = inside(2 - 4 * core)
    from_partner = core == side

    def column(g, width):
        return pl.ds(pl.multiple_of(g * width, width), width)

    def remote(src, dst, sent, received, device):
        if not COMM:
            return Nop()
        return pltpu.make_async_remote_copy(
            src_ref=src, dst_ref=dst, send_sem=sent, recv_sem=received,
            device_id=device, device_id_type=pl.DeviceIdType.MESH,
        )

    def near_copy(g, source, slot, kind, device):
        return remote(source, near.at[g, slot], near_send.at[g, kind], near_recv.at[g, slot], device)

    def partner_copy(g):
        return near_copy(g, kv.at[g], 3 * side, 0, partner)

    def beside_copy(g):
        return near_copy(g, kv.at[g], 1 + core, 1, sibling)

    def diag_copy(g):
        return near_copy(g, kv.at[g], 3 - 3 * side, 2, diagonal)

    def ahead_copy(g):
        return near_copy(g, near.at[g, partner_slot], diag_slot, 2, ahead)

    def relay_copy(g):
        return near_copy(g, near.at[g, forward], 2 - core, 3, sibling)

    def near_wait(g, slot):
        near_copy(g, near.at[g, slot], slot, 0, sibling).wait_recv()

    def grad_copy(g, slot, place, kind, device):
        if not GCOMM:
            return Nop()
        return remote(gsend.at[g, slot], grecv.at[g, place], grad_send.at[g, kind], grad_recv.at[g, place], device)

    def beside_grad(g):
        return grad_copy(g, beside, 0, 0, sibling)

    def passed_grad(g):
        return grad_copy(g, passed, 1, 1, sibling)

    def behind_grad(g):
        return grad_copy(g, diag_slot, 2, 2, behind)

    def partner_grad(g):
        return grad_copy(g, partner_slot, 3, 3, partner)

    def diag_grad(g):
        return grad_copy(g, diag_slot, 4, 2, diagonal)

    def kv_load(g, part):
        return pltpu.make_async_copy(
            kv_hbm.at[:, pl.ds(part * kv_width + g * HEAD, HEAD)], kv.at[g, part], kv_sem.at[g, part]
        )

    def load_copies(g):
        return (
            pltpu.make_async_copy(q_hbm.at[:, column(g, wide)], q.at[:, column(g, wide)], in_sem.at[g, 0]),
            pltpu.make_async_copy(do_hbm.at[:, column(g, wide)], do.at[:, column(g, wide)], in_sem.at[g, 1]),
        )

    for g in range(groups):
        for part in range(2):
            kv_load(g, part).start()
    for copy in load_copies(0):
        copy.start()
    barrier = pltpu.get_barrier_semaphore()

    def greet(device):
        pl.semaphore_signal(barrier, inc=1, device_id=device, device_id_type=pl.DeviceIdType.MESH)

    greet(partner)
    greet(sibling)

    @pl.when(has_ahead)
    def _():
        greet(ahead)

    @pl.when(has_behind)
    def _():
        greet(behind)
        if KV_DIRECT or GRAD_DIRECT:
            greet(diagonal)

    for g in range(1, groups):
        for copy in load_copies(g):
            copy.start()

    for o in range(4):

        @pl.when(jnp.logical_not(exists(o)))
        def _():
            near[:, o] = jnp.zeros((groups, 2, rows, HEAD), near.dtype)

    @pl.when(jnp.logical_not(has_behind))
    def _():
        for g in range(groups):
            if g in GRAD_DIRECT:
                grecv[g, 4] = jnp.zeros((2, rows, HEAD), grecv.dtype)

    for g in range(groups):
        kv_load(g, 0).wait()
        kv_load(g, 1).wait()
    pl.semaphore_wait(barrier, 2 + has_ahead.astype(jnp.int32) + PEERS * has_behind.astype(jnp.int32))

    for g in range(groups):
        if g in KV_DIRECT:

            @pl.when(has_behind)
            def _():
                diag_copy(g).start()

        partner_copy(g).start()
        beside_copy(g).start()

    own_block = slot_ref[me]
    live_count = count_ref[own_block]
    chosen = []
    bias = []
    for j in (1, 2):
        wanted = blocks_ref[j, own_block]
        hits = []
        for o in range(4):
            there = jnp.clip(me + OFFSETS[o], 0, n - 1)
            hits.append(exists(o) & (slot_ref[there] == wanted) & (live_count > j))
        chosen.append(hits)
        bias.append(jnp.where(hits[0] | hits[1] | hits[2] | hits[3], 0.0, NEG).astype(jnp.float32))

    def pick(g, part, hits):
        value = near[g, 0, part]
        for o in range(1, 4):
            value = jnp.where(hits[o], near[g, o, part], value)
        return value

    def from_diag(g):
        @pl.when(has_behind)
        def _():
            near_wait(g, diag_slot)

            @pl.when(jnp.logical_not(from_partner))
            def _():
                relay_copy(g).start()

    def combine(g):
        @pl.when(has_forward)
        def _():
            passed_grad(g).wait_recv()
            both = gsend[g, forward].astype(jnp.float32) + grecv[g, 1].astype(jnp.float32)
            gsend[g, forward] = both.astype(jnp.bfloat16)

        send_diag(g, jnp.logical_not(from_partner))
        send_partner(g, from_partner)

    def send_diag(g, mine):
        mine = jnp.logical_and(mine, has_behind)
        direct = among(g, GRAD_DIRECT)

        @pl.when(jnp.logical_and(mine, direct))
        def _():
            diag_grad(g).start()

        @pl.when(jnp.logical_and(mine, jnp.logical_not(direct)))
        def _():
            behind_grad(g).start()

    def send_partner(g, mine):
        direct = among(g, GRAD_DIRECT)

        @pl.when(jnp.logical_and(mine, jnp.logical_or(direct, jnp.logical_not(has_ahead))))
        def _():
            partner_grad(g).start()

    def add_ahead(g):
        @pl.when(jnp.logical_and(has_ahead, jnp.logical_not(among(g, GRAD_DIRECT))))
        def _():
            grad_copy(g, 0, 2, 0, sibling).wait_recv()
            both = gsend[g, partner_slot].astype(jnp.float32) + grecv[g, 2].astype(jnp.float32)
            gsend[g, partner_slot] = both.astype(jnp.bfloat16)
            partner_grad(g).start()

    def at(index, pred, action):
        pl.when(pred)(functools.partial(action, index))

    def step(g, carry):
        for copy in load_copies(g):
            copy.wait()
        near_wait(g, beside)

        @pl.when(has_passed)
        def _():
            near_wait(g, passed)

        picked[g, 0] = jnp.concatenate([kv[g, 0], pick(g, 0, chosen[0]), pick(g, 0, chosen[1])], axis=0)
        picked[g, 1] = jnp.concatenate([kv[g, 1], pick(g, 1, chosen[0]), pick(g, 1, chosen[1])], axis=0)
        keys = picked[g, 0]
        values = picked[g, 1]
        heads = [pl.multiple_of(g * wide + h * HEAD, HEAD) for h in range(repeats)]

        def matmuls(pair):
            q2 = jnp.concatenate([q[:, pl.ds(heads[2 * pair + i], HEAD)] for i in range(2)], axis=0)
            do2 = jnp.concatenate([do[:, pl.ds(heads[2 * pair + i], HEAD)] for i in range(2)], axis=0)
            score[pair % DEPTH] = lax.dot_general(keys, q2, NT, preferred_element_type=jnp.float32)
            pgrad[pair % DEPTH] = lax.dot_general(values, do2, NT, preferred_element_type=jnp.float32)

        def softmax(pair):
            for i in range(2):
                lanes = pl.ds(i * rows, rows)
                tops = []
                for j in range(3):
                    top = jnp.max(score[pair % DEPTH, pl.ds(j * rows, rows), lanes], axis=0, keepdims=True)
                    tops.append(top if j == 0 else top + bias[j - 1])
                best = jnp.maximum(jnp.maximum(tops[0], tops[1]), tops[2]) * (scale * LOG2E)
                total = jnp.zeros((8, rows), jnp.float32)
                dot = jnp.zeros((8, rows), jnp.float32)
                for j in range(3):
                    shift = best if j == 0 else best - bias[j - 1]
                    for c in range(0, rows, CHUNK):
                        at_rows = pl.ds(j * rows + c, CHUNK)
                        weight = jnp.exp2(score[pair % DEPTH, at_rows, lanes] * (scale * LOG2E) - shift)
                        score[pair % DEPTH, at_rows, lanes] = weight
                        total = total + jnp.sum(weight.reshape(CHUNK // 8, 8, rows), axis=0)
                        both = weight * pgrad[pair % DEPTH, at_rows, lanes]
                        dot = dot + jnp.sum(both.reshape(CHUNK // 8, 8, rows), axis=0)
                inverse = 1.0 / jnp.sum(total, axis=0, keepdims=True)
                delta = jnp.sum(dot, axis=0, keepdims=True) * inverse
                where = pl.ds((2 * pair + i) * HEAD, HEAD)
                for c in range(0, 3 * rows, CHUNK):
                    at_rows = pl.ds(c, CHUNK)
                    prob = score[pair % DEPTH, at_rows, lanes] * inverse
                    probs[g, at_rows, where] = prob.astype(jnp.bfloat16)
                    dscores[g, at_rows, where] = (prob * (pgrad[pair % DEPTH, at_rows, lanes] - delta)).astype(jnp.bfloat16)

        def sums(first, last):
            part = pl.ds(first * HEAD, (last - first) * HEAD)
            q_all = jnp.concatenate([q[:, pl.ds(heads[h], HEAD)] for h in range(first, last)], axis=0)
            do_all = jnp.concatenate([do[:, pl.ds(heads[h], HEAD)] for h in range(first, last)], axis=0)
            return (
                jnp.dot(dscores[g, :, part], q_all, preferred_element_type=jnp.float32),
                jnp.dot(probs[g, :, part], do_all, preferred_element_type=jnp.float32),
            )

        if COMP:
            matmuls(0)
            matmuls(1)
            softmax(0)
            if DEPTH > 2:
                matmuls(2)
            softmax(1)
        at(g - 1, g > 0, combine)
        at(g + 1, g + 1 < groups, from_diag)
        if COMP:
            if DEPTH <= 2:
                matmuls(2)
            matmuls(3)
            softmax(2)
            softmax(3)
            key_grad, value_grad = sums(0, repeats)
        else:
            key_grad = jnp.zeros((3 * rows, HEAD), jnp.float32)
            value_grad = jnp.zeros((3 * rows, HEAD), jnp.float32)
        at(g - 2, g > 1, add_ahead)
        for part, grad in ((0, key_grad * scale), (1, value_grad)):
            own_grad[g, part] = grad[:rows]
            for o in range(4):
                gsend[g, o, part] = jnp.where(
                    chosen[0][o], grad[rows : 2 * rows], jnp.where(chosen[1][o], grad[2 * rows :], 0.0)
                ).astype(jnp.bfloat16)

        @pl.when(has_passed)
        def _():
            passed_grad(g).start()

        send_diag(g, from_partner)
        send_partner(g, jnp.logical_not(from_partner))
        beside_grad(g).start()
        return carry

    def results(g, carry):
        keys_t = picked[g, 0].T
        values_t = picked[g, 1].T
        for pair in range(pairs):
            if COMP:
                part = pl.ds(2 * pair * HEAD, 2 * HEAD)
                mixed = jnp.dot(values_t, probs[g, :, part], preferred_element_type=jnp.float32)
                query_grad = jnp.dot(keys_t, dscores[g, :, part], preferred_element_type=jnp.float32) * scale
                mixed = mixed.astype(jnp.bfloat16).T
                query_grad = query_grad.astype(jnp.bfloat16).T
                for i in range(2):
                    where = pl.ds(pl.multiple_of(g * wide + (2 * pair + i) * HEAD, HEAD), HEAD)
                    att[:, where] = mixed[i * rows : (i + 1) * rows]
                    dq[:, where] = query_grad[i * rows : (i + 1) * rows]
        at(groups - 1, g == 0, combine)
        at(groups - 2, g == 1, add_ahead)
        return carry

    for g in range(groups):
        if g == EARLY:
            from_diag(0)
        near_wait(g, partner_slot)
        if g not in KV_DIRECT:

            @pl.when(has_ahead)
            def _():
                ahead_copy(g).start()

        @pl.when(from_partner)
        def _():
            relay_copy(g).start()

    if EARLY >= groups:
        from_diag(0)
    lax.fori_loop(0, groups, step, 0)
    lax.fori_loop(0, groups, results, 0)
    add_ahead(groups - 1)

    def finish(g, carry):
        beside_grad(g).wait_recv()
        grad_copy(g, 0, 3, 0, partner).wait_recv()
        direct = among(g, GRAD_DIRECT)

        @pl.when(jnp.logical_and(direct, has_behind))
        def _():
            grad_copy(g, 0, 4, 0, partner).wait_recv()

        for part in range(2):
            total = own_grad[g, part]
            total = total + grecv[g, 0, part].astype(jnp.float32)
            total = total + grecv[g, 3, part].astype(jnp.float32)
            where = pl.ds(pl.multiple_of(part * kv_width + g * HEAD, HEAD), HEAD)

            @pl.when(direct)
            def _():
                kvg[:, where] = (total + grecv[g, 4, part].astype(jnp.float32)).astype(jnp.bfloat16)

            @pl.when(jnp.logical_not(direct))
            def _():
                kvg[:, where] = total.astype(jnp.bfloat16)

        return carry

    lax.fori_loop(0, groups, finish, 0)

    def drain(g, carry):
        partner_copy(g).wait_send()
        beside_copy(g).wait_send()
        direct = among(g, KV_DIRECT)

        @pl.when(jnp.logical_and(direct, has_behind))
        def _():
            diag_copy(g).wait_send()

        @pl.when(jnp.logical_and(jnp.logical_not(direct), has_ahead))
        def _():
            ahead_copy(g).wait_send()

        @pl.when(has_forward)
        def _():
            relay_copy(g).wait_send()

        beside_grad(g).wait_send()
        partner_grad(g).wait_send()

        @pl.when(has_passed)
        def _():
            passed_grad(g).wait_send()

        @pl.when(has_behind)
        def _():
            behind_grad(g).wait_send()

        return carry

    lax.fori_loop(0, groups, drain, 0)


def flush(att, dq, kvg, att_out, dq_out, kvg_out, out_sem):
    width = kvg.shape[1]
    pieces = [(kvg, kvg_out, 0)]
    for start in range(0, att.shape[1], width):
        pieces.append((att, att_out, start))
        pieces.append((dq, dq_out, start))
    stores = []
    for i, (source, result, start) in enumerate(pieces):
        part = pl.ds(start, width)
        stores.append(pltpu.make_async_copy(source.at[:, part], result.at[:, part], out_sem.at[i]))
    for store in stores:
        store.start()
    for store in stores:
        store.wait()


def body(queries, keys_values, out_grad, key_blocks, key_count, block_at_slot):
    n = lax.axis_size("ctx")
    rows, width = queries.shape
    kv_width = keys_values.shape[1] // 2
    groups = kv_width // HEAD
    repeats = width // kv_width
    scalars = pl.BlockSpec(memory_space=pltpu.SMEM)
    wide = pltpu.VMEM((rows, width), jnp.bfloat16)
    narrow = pltpu.VMEM((rows, 2 * kv_width), jnp.bfloat16)
    dma = pltpu.SemaphoreType.DMA
    shapes = (
        jax.ShapeDtypeStruct((rows, width), jnp.bfloat16),
        jax.ShapeDtypeStruct((rows, width), jnp.bfloat16),
        jax.ShapeDtypeStruct((rows, 2 * kv_width), jnp.bfloat16),
    )

    def blocks(*lead, dtype=jnp.bfloat16):
        return pltpu.VMEM((*lead, rows, HEAD), dtype)

    pieces = 2 * (width // (2 * kv_width)) + 1
    held = pl.BlockSpec(memory_space=pltpu.VMEM)
    pair_wide = pltpu.VMEM((groups, 3 * rows, repeats * rows), jnp.bfloat16)
    pair_float = pltpu.VMEM((DEPTH, 3 * rows, 2 * rows), jnp.float32)
    results = pl.pallas_call(
        functools.partial(kernel, n, groups, repeats),
        out_shape=(wide, wide, narrow),
        in_specs=[scalars] * 3 + [pl.BlockSpec(memory_space=pltpu.HBM)] * 3,
        out_specs=(held, held, held),
        scratch_shapes=[
            wide, blocks(groups, 2), wide, blocks(groups, 4, 2),
            pltpu.VMEM((groups, 2, 3 * rows, HEAD), jnp.bfloat16), pair_wide, pair_wide, pair_float, pair_float,
            blocks(groups, 2, dtype=jnp.float32), blocks(groups, 4, 2), blocks(groups, 5, 2),
            dma((groups, 2)), dma((groups, 2)),
            dma((groups, 4)), dma((groups, 4)), dma((groups, 4)), dma((groups, 5)),
        ],
        compiler_params=pltpu.CompilerParams(
            collective_id=0, has_side_effects=True, vmem_limit_bytes=61 * 1024 * 1024
        ),
    )(key_blocks.T, key_count, block_at_slot, queries, keys_values, out_grad)
    return pl.pallas_call(
        flush,
        out_shape=shapes,
        in_specs=[held] * 3,
        out_specs=(pl.BlockSpec(memory_space=pltpu.HBM),) * 3,
        scratch_shapes=[dma((pieces,))],
        compiler_params=pltpu.CompilerParams(vmem_limit_bytes=16 * 1024 * 1024),
    )(*results)


def solution(mesh):
    sharded = P(("groups", "ctx"), None)
    return jax.shard_map(
        body,
        mesh=mesh,
        in_specs=(sharded, sharded, sharded, P("groups", None), P("groups"), P("groups")),
        out_specs=(sharded, sharded, sharded),
        check_vma=False,
    )
```

```python
import functools

import jax
import jax.numpy as jnp
from jax import lax
from jax.experimental import pallas as pl
from jax.experimental.pallas import tpu as pltpu
from jax.sharding import PartitionSpec as P

HEAD = 128
OFFSETS = (-2, -1, 1, 2)
LOG2E = 1.4426950408889634
NEG = -1e30
NT = (((1,), (1,)), ((), ()))
KV_DIRECT = ()
GRAD_DIRECT = (0,1,2)
COMM = True
SPLIT = True
PEERS = 1
GCOMM = True
CHUNK = 32
DEPTH = 2
COMP = True


class Nop:
    def start(self):
        pass

    def wait_send(self):
        pass

    def wait_recv(self):
        pass


def among(g, members):
    if isinstance(g, int):
        return g in members
    found = jnp.bool_(False)
    for m in members:
        found = jnp.logical_or(found, g == m)
    return found


def kernel(
    n, groups, repeats,
    blocks_ref, count_ref, slot_ref, q_hbm, kv_hbm, do_hbm,
    att, dq, kvg,
    q, kv, do, near, picked, score, pgrad, stats, own_grad, gsend, grecv,
    in_sem, kv_sem, near_send, near_recv, grad_send, grad_recv,
):
    rows = q.shape[0]
    wide = repeats * HEAD
    kv_width = groups * HEAD
    pairs = repeats // 2
    scale = HEAD ** (-0.5)
    me = lax.axis_index("ctx")
    core = lax.rem(me, 2)
    side = lax.rem(me // 2, 2)
    along = 4 - 8 * side

    def inside(d):
        return jnp.logical_and(me + d >= 0, me + d < n)

    def exists(o):
        return inside(OFFSETS[o])

    sibling = {"ctx": me + 1 - 2 * core}
    partner = {"ctx": me + 2 - 4 * side}
    diagonal = {"ctx": me - 2 + 4 * side}
    ahead = {"ctx": me + along}
    behind = {"ctx": me - along}
    has_ahead = inside(along)
    has_behind = inside(-along)
    partner_slot = 3 - 3 * side
    diag_slot = 3 * side
    forward = 3 * (1 - core)
    free = 3 * core
    passed = 1 + core
    beside = 2 - core
    has_passed = inside(2 * core - 1)
    has_forward = inside(2 - 4 * core)
    from_partner = core == side

    def column(g, width):
        return pl.ds(pl.multiple_of(g * width, width), width)

    def remote(src, dst, sent, received, device):
        if not COMM:
            return Nop()
        return pltpu.make_async_remote_copy(
            src_ref=src, dst_ref=dst, send_sem=sent, recv_sem=received,
            device_id=device, device_id_type=pl.DeviceIdType.MESH,
        )

    def near_copy(g, part, source, slot, kind, device):
        return remote(
            source.at[part], near.at[g, slot, part], near_send.at[g, kind, part], near_recv.at[g, slot, part], device
        )

    def partner_copy(g, part):
        return near_copy(g, part, kv.at[g], 3 * side, 0, partner)

    def beside_copy(g, part):
        return near_copy(g, part, kv.at[g], 1 + core, 1, sibling)

    def diag_copy(g, part):
        return near_copy(g, part, kv.at[g], 3 - 3 * side, 2, diagonal)

    def ahead_copy(g, part):
        return near_copy(g, part, near.at[g, partner_slot], diag_slot, 2, ahead)

    def relay_copy(g, part):
        return near_copy(g, part, near.at[g, forward], 2 - core, 3, sibling)

    def near_wait(g, part, slot):
        near_copy(g, part, near.at[g, slot], slot, 0, sibling).wait_recv()

    def grad_copy(g, part, slot, place, kind, device):
        if not GCOMM:
            return Nop()
        return remote(
            gsend.at[g, slot, part], grecv.at[g, place, part],
            grad_send.at[g, kind, part], grad_recv.at[g, place, part], device,
        )

    def beside_grad(g, part):
        return grad_copy(g, part, beside, 0, 0, sibling)

    def passed_grad(g, part):
        return grad_copy(g, part, passed, 1, 1, sibling)

    def behind_grad(g, part):
        return grad_copy(g, part, diag_slot, 2, 2, behind)

    def partner_grad(g, part):
        return grad_copy(g, part, partner_slot, 3, 3, partner)

    def diag_grad(g, part):
        return grad_copy(g, part, diag_slot, 4, 2, diagonal)

    def kv_load(g, part):
        return pltpu.make_async_copy(
            kv_hbm.at[:, pl.ds(part * kv_width + g * HEAD, HEAD)], kv.at[g, part], kv_sem.at[g, part]
        )

    def load_copies(g):
        return (
            pltpu.make_async_copy(q_hbm.at[:, column(g, wide)], q.at[:, column(g, wide)], in_sem.at[g, 0]),
            pltpu.make_async_copy(do_hbm.at[:, column(g, wide)], do.at[:, column(g, wide)], in_sem.at[g, 1]),
        )

    for g in range(groups):
        for part in range(2):
            kv_load(g, part).start()
    for copy in load_copies(0):
        copy.start()
    barrier = pltpu.get_barrier_semaphore()

    def greet(device):
        pl.semaphore_signal(barrier, inc=1, device_id=device, device_id_type=pl.DeviceIdType.MESH)

    greet(partner)
    greet(sibling)

    @pl.when(has_ahead)
    def _():
        greet(ahead)

    @pl.when(has_behind)
    def _():
        greet(behind)
        if PEERS > 1:
            greet(diagonal)

    for g in range(1, groups):
        for copy in load_copies(g):
            copy.start()

    for o in range(4):

        @pl.when(jnp.logical_not(exists(o)))
        def _():
            near[:, o] = jnp.zeros((groups, 2, rows, HEAD), near.dtype)

    @pl.when(jnp.logical_not(has_behind))
    def _():
        for g in range(groups):
            if g in GRAD_DIRECT:
                grecv[g, 4] = jnp.zeros((2, rows, HEAD), grecv.dtype)

    for g in range(groups):
        kv_load(g, 0).wait()
        kv_load(g, 1).wait()
    pl.semaphore_wait(barrier, 2 + has_ahead.astype(jnp.int32) + PEERS * has_behind.astype(jnp.int32))

    for g in range(groups):
        for part in range(2):
            if g in KV_DIRECT:

                @pl.when(has_behind)
                def _():
                    diag_copy(g, part).start()

            partner_copy(g, part).start()
        for part in range(2):
            beside_copy(g, part).start()

    own_block = slot_ref[me]
    live_count = count_ref[own_block]
    chosen = []
    bias = []
    for j in (1, 2):
        wanted = blocks_ref[j, own_block]
        hits = []
        for o in range(4):
            there = jnp.clip(me + OFFSETS[o], 0, n - 1)
            hits.append(exists(o) & (slot_ref[there] == wanted) & (live_count > j))
        chosen.append(hits)
        bias.append(jnp.where(hits[0] | hits[1] | hits[2] | hits[3], 0.0, NEG).astype(jnp.float32))

    def pick(g, part, hits):
        value = near[g, 0, part]
        for o in range(1, 4):
            value = jnp.where(hits[o], near[g, o, part], value)
        return value

    def from_diag(g):
        @pl.when(has_behind)
        def _():
            for part in range(2):
                near_wait(g, part, diag_slot)

                @pl.when(jnp.logical_not(from_partner))
                def _():
                    relay_copy(g, part).start()

    def plus(g, part, slot, place):
        both = gsend[g, slot, part].astype(jnp.float32) + grecv[g, place, part].astype(jnp.float32)
        gsend[g, slot, part] = both.astype(jnp.bfloat16)

    def combine(g):
        for part in range(2):

            @pl.when(has_forward)
            def _():
                passed_grad(g, part).wait_recv()
                plus(g, part, forward, 1)

            send_diag(g, part, jnp.logical_not(from_partner))
            send_partner(g, part, from_partner)

    def send_diag(g, part, mine):
        mine = jnp.logical_and(mine, has_behind)
        direct = among(g, GRAD_DIRECT)

        @pl.when(jnp.logical_and(mine, direct))
        def _():
            diag_grad(g, part).start()

        @pl.when(jnp.logical_and(mine, jnp.logical_not(direct)))
        def _():
            behind_grad(g, part).start()

    def send_partner(g, part, mine):
        direct = among(g, GRAD_DIRECT)

        @pl.when(jnp.logical_and(mine, jnp.logical_or(direct, jnp.logical_not(has_ahead))))
        def _():
            partner_grad(g, part).start()

    def add_ahead(g):
        @pl.when(jnp.logical_and(has_ahead, jnp.logical_not(among(g, GRAD_DIRECT))))
        def _():
            for part in range(2):
                grad_copy(g, part, 0, 2, 0, sibling).wait_recv()
                plus(g, part, partner_slot, 2)
                partner_grad(g, part).start()

    def at(index, pred, action):
        pl.when(pred)(functools.partial(action, index))

    def step(g, carry):
        for copy in load_copies(g):
            copy.wait()
        for part in range(2):
            near_wait(g, part, beside)

        @pl.when(has_passed)
        def _():
            for part in range(2):
                near_wait(g, part, passed)

        picked[g, 0] = jnp.concatenate([kv[g, 0], pick(g, 0, chosen[0]), pick(g, 0, chosen[1])], axis=0)
        picked[g, 1] = jnp.concatenate([kv[g, 1], pick(g, 1, chosen[0]), pick(g, 1, chosen[1])], axis=0)
        keys = picked[g, 0]
        values = picked[g, 1]
        heads = [pl.multiple_of(g * wide + h * HEAD, HEAD) for h in range(repeats)]

        def stacked(source, pair):
            return jnp.concatenate([source[:, pl.ds(heads[2 * pair + i], HEAD)] for i in range(2)], axis=0)

        def matmuls(pair):
            raw = lax.dot_general(keys, stacked(q, pair), NT, preferred_element_type=jnp.float32)
            tops = []
            for j in range(3):
                top = jnp.max(raw[j * rows : (j + 1) * rows], axis=0, keepdims=True)
                tops.append(top if j == 0 else top + bias[j - 1])
            score[g, pair] = raw
            pgrad[g, pair] = lax.dot_general(values, stacked(do, pair), NT, preferred_element_type=jnp.float32)
            return jnp.maximum(jnp.maximum(tops[0], tops[1]), tops[2]) * (scale * LOG2E)

        def softmax(pair, best):
            total = jnp.zeros((8, 2 * rows), jnp.float32)
            dot = jnp.zeros((8, 2 * rows), jnp.float32)
            for j in range(3):
                shift = best if j == 0 else best - bias[j - 1]
                for c in range(0, rows, CHUNK):
                    at_rows = pl.ds(j * rows + c, CHUNK)
                    weight = jnp.exp2(score[g, pair, at_rows] * (scale * LOG2E) - shift)
                    score[g, pair, at_rows] = weight
                    total = total + jnp.sum(weight.reshape(CHUNK // 8, 8, 2 * rows), axis=0)
                    both = weight * pgrad[g, pair, at_rows]
                    dot = dot + jnp.sum(both.reshape(CHUNK // 8, 8, 2 * rows), axis=0)
            inverse = 1.0 / jnp.sum(total, axis=0, keepdims=True)
            delta = jnp.sum(dot, axis=0, keepdims=True) * inverse
            stats[g, pair, 0:1] = inverse
            stats[g, pair, 1:2] = delta
            return inverse, delta

        def sums(pair, inverse, delta, key_grad, value_grad):
            prob = score[g, pair] * inverse
            score_grads = (prob * (pgrad[g, pair] - delta)).astype(jnp.bfloat16)
            rounded = prob.astype(jnp.bfloat16)
            return (
                key_grad + jnp.dot(score_grads, stacked(q, pair), preferred_element_type=jnp.float32),
                value_grad + jnp.dot(rounded, stacked(do, pair), preferred_element_type=jnp.float32),
            )

        key_grad = jnp.zeros((3 * rows, HEAD), jnp.float32)
        value_grad = jnp.zeros((3 * rows, HEAD), jnp.float32)
        if COMP:
            best0 = matmuls(0)
            best1 = matmuls(1)
            stat0 = softmax(0, best0)
            best2 = matmuls(2)
            key_grad, value_grad = sums(0, *stat0, key_grad, value_grad)
            stat1 = softmax(1, best1)
        at(g - 1, g > 0, combine)
        at(g + 1, g + 1 < groups, from_diag)
        if COMP:
            best3 = matmuls(3)
            key_grad, value_grad = sums(1, *stat1, key_grad, value_grad)
            stat2 = softmax(2, best2)
            key_grad, value_grad = sums(2, *stat2, key_grad, value_grad)
            stat3 = softmax(3, best3)
            key_grad, value_grad = sums(3, *stat3, key_grad, value_grad)
        for part, grad in ((0, key_grad * scale), (1, value_grad)):
            own_grad[g, part] = grad[:rows]
            for o in range(4):
                gsend[g, o, part] = jnp.where(
                    chosen[0][o], grad[rows : 2 * rows], jnp.where(chosen[1][o], grad[2 * rows :], 0.0)
                ).astype(jnp.bfloat16)

        for part in range(2):

            @pl.when(has_passed)
            def _():
                passed_grad(g, part).start()

            send_diag(g, part, from_partner)
            send_partner(g, part, jnp.logical_not(from_partner))
        for part in range(2):
            beside_grad(g, part).start()
        return carry

    def results(g, carry):
        keys_t = picked[g, 0].T
        values_t = picked[g, 1].T
        for pair in range(pairs):
            if COMP:
                prob = score[g, pair] * stats[g, pair, 0:1]
                score_grads = (prob * (pgrad[g, pair] - stats[g, pair, 1:2])).astype(jnp.bfloat16)
                mixed = jnp.dot(values_t, prob.astype(jnp.bfloat16), preferred_element_type=jnp.float32)
                query_grad = jnp.dot(keys_t, score_grads, preferred_element_type=jnp.float32) * scale
                mixed = mixed.astype(jnp.bfloat16).T
                query_grad = query_grad.astype(jnp.bfloat16).T
                for i in range(2):
                    where = pl.ds(pl.multiple_of(g * wide + (2 * pair + i) * HEAD, HEAD), HEAD)
                    att[:, where] = mixed[i * rows : (i + 1) * rows]
                    dq[:, where] = query_grad[i * rows : (i + 1) * rows]
        at(groups - 1, g == 0, combine)
        at(g + 1, g + 2 < groups, add_ahead)
        return carry

    for g in range(groups):
        for part in range(2):
            near_wait(g, part, partner_slot)
            if g not in KV_DIRECT:

                @pl.when(has_ahead)
                def _():
                    ahead_copy(g, part).start()

            @pl.when(from_partner)
            def _():
                relay_copy(g, part).start()

    from_diag(0)
    lax.fori_loop(0, groups, step, 0)
    add_ahead(0)
    lax.fori_loop(0, groups, results, 0)
    add_ahead(groups - 1)

    def finish(g, carry):
        direct = among(g, GRAD_DIRECT)
        for part in range(2):
            beside_grad(g, part).wait_recv()
            total = own_grad[g, part] + grecv[g, 0, part].astype(jnp.float32)
            where = pl.ds(pl.multiple_of(part * kv_width + g * HEAD, HEAD), HEAD)

            @pl.when(jnp.logical_and(direct, has_behind))
            def _():
                grad_copy(g, part, 0, 4, 0, partner).wait_recv()

            grad_copy(g, part, 0, 3, 0, partner).wait_recv()
            total = total + grecv[g, 3, part].astype(jnp.float32)

            @pl.when(direct)
            def _():
                kvg[:, where] = (total + grecv[g, 4, part].astype(jnp.float32)).astype(jnp.bfloat16)

            @pl.when(jnp.logical_not(direct))
            def _():
                kvg[:, where] = total.astype(jnp.bfloat16)

        return carry

    lax.fori_loop(0, groups, finish, 0)

    def drain(g, carry):
        direct = among(g, KV_DIRECT)
        for part in range(2):
            partner_copy(g, part).wait_send()
            beside_copy(g, part).wait_send()

            @pl.when(jnp.logical_and(direct, has_behind))
            def _():
                diag_copy(g, part).wait_send()

            @pl.when(jnp.logical_and(jnp.logical_not(direct), has_ahead))
            def _():
                ahead_copy(g, part).wait_send()

            @pl.when(has_forward)
            def _():
                relay_copy(g, part).wait_send()

            beside_grad(g, part).wait_send()
            partner_grad(g, part).wait_send()

            @pl.when(has_passed)
            def _():
                passed_grad(g, part).wait_send()

            @pl.when(has_behind)
            def _():
                behind_grad(g, part).wait_send()

        return carry

    lax.fori_loop(0, groups, drain, 0)


def flush(att, dq, kvg, att_out, dq_out, kvg_out, out_sem):
    width = kvg.shape[1]
    pieces = [(kvg, kvg_out, 0)]
    for start in range(0, att.shape[1], width):
        pieces.append((att, att_out, start))
        pieces.append((dq, dq_out, start))
    stores = []
    for i, (source, result, start) in enumerate(pieces):
        part = pl.ds(start, width)
        stores.append(pltpu.make_async_copy(source.at[:, part], result.at[:, part], out_sem.at[i]))
    for store in stores:
        store.start()
    for store in stores:
        store.wait()


def body(queries, keys_values, out_grad, key_blocks, key_count, block_at_slot):
    n = lax.axis_size("ctx")
    rows, width = queries.shape
    kv_width = keys_values.shape[1] // 2
    groups = kv_width // HEAD
    repeats = width // kv_width
    scalars = pl.BlockSpec(memory_space=pltpu.SMEM)
    wide = pltpu.VMEM((rows, width), jnp.bfloat16)
    narrow = pltpu.VMEM((rows, 2 * kv_width), jnp.bfloat16)
    dma = pltpu.SemaphoreType.DMA
    shapes = (
        jax.ShapeDtypeStruct((rows, width), jnp.bfloat16),
        jax.ShapeDtypeStruct((rows, width), jnp.bfloat16),
        jax.ShapeDtypeStruct((rows, 2 * kv_width), jnp.bfloat16),
    )

    def blocks(*lead, dtype=jnp.bfloat16):
        return pltpu.VMEM((*lead, rows, HEAD), dtype)

    pieces = 2 * (width // (2 * kv_width)) + 1
    held = pl.BlockSpec(memory_space=pltpu.VMEM)
    pair_float = pltpu.VMEM((groups, repeats // 2, 3 * rows, 2 * rows), jnp.float32)
    pair_stats = pltpu.VMEM((groups, repeats // 2, 8, 2 * rows), jnp.float32)
    results = pl.pallas_call(
        functools.partial(kernel, n, groups, repeats),
        out_shape=(wide, wide, narrow),
        in_specs=[scalars] * 3 + [pl.BlockSpec(memory_space=pltpu.HBM)] * 3,
        out_specs=(held, held, held),
        scratch_shapes=[
            wide, blocks(groups, 2), wide, blocks(groups, 4, 2),
            pltpu.VMEM((groups, 2, 3 * rows, HEAD), jnp.bfloat16), pair_float, pair_float, pair_stats,
            blocks(groups, 2, dtype=jnp.float32), blocks(groups, 4, 2), blocks(groups, 5, 2),
            dma((groups, 2)), dma((groups, 2)),
            dma((groups, 4, 2)), dma((groups, 4, 2)), dma((groups, 4, 2)), dma((groups, 5, 2)),
        ],
        compiler_params=pltpu.CompilerParams(
            collective_id=0, has_side_effects=True, vmem_limit_bytes=61 * 1024 * 1024
        ),
    )(key_blocks.T, key_count, block_at_slot, queries, keys_values, out_grad)
    return pl.pallas_call(
        flush,
        out_shape=shapes,
        in_specs=[held] * 3,
        out_specs=(pl.BlockSpec(memory_space=pltpu.HBM),) * 3,
        scratch_shapes=[dma((pieces,))],
        compiler_params=pltpu.CompilerParams(vmem_limit_bytes=16 * 1024 * 1024),
    )(*results)


def solution(mesh):
    sharded = P(("groups", "ctx"), None)
    return jax.shard_map(
        body,
        mesh=mesh,
        in_specs=(sharded, sharded, sharded, P("groups", None), P("groups"), P("groups")),
        out_specs=(sharded, sharded, sharded),
        check_vma=False,
    )
```

```python
import functools

import jax
import jax.numpy as jnp
from jax import lax
from jax.experimental import pallas as pl
from jax.experimental.pallas import tpu as pltpu
from jax.sharding import PartitionSpec as P

HEAD = 128
OFFSETS = (-2, -1, 1, 2)
LOG2E = 1.4426950408889634
NEG = -1e30
NT = (((1,), (1,)), ((), ()))
KV_DIRECT = ()
GRAD_DIRECT = (0,1,2)
CHUNK = 32


def among(g, members):
    if isinstance(g, int):
        return g in members
    found = jnp.bool_(False)
    for m in members:
        found = jnp.logical_or(found, g == m)
    return found


def kernel(
    n, groups, repeats,
    blocks_ref, count_ref, slot_ref, q_hbm, kv_hbm, do_hbm,
    att, dq, kvg,
    q, kv, do, near, picked, score, pgrad, stats, own_grad, gsend, grecv,
    in_sem, kv_sem, near_send, near_recv, grad_send, grad_recv,
):
    rows = q.shape[0]
    wide = repeats * HEAD
    kv_width = groups * HEAD
    pairs = repeats // 2
    scale = HEAD ** (-0.5)
    me = lax.axis_index("ctx")
    core = lax.rem(me, 2)
    side = lax.rem(me // 2, 2)
    along = 4 - 8 * side

    def inside(d):
        return jnp.logical_and(me + d >= 0, me + d < n)

    def exists(o):
        return inside(OFFSETS[o])

    sibling = {"ctx": me + 1 - 2 * core}
    partner = {"ctx": me + 2 - 4 * side}
    diagonal = {"ctx": me - 2 + 4 * side}
    ahead = {"ctx": me + along}
    behind = {"ctx": me - along}
    has_ahead = inside(along)
    has_behind = inside(-along)
    partner_slot = 3 - 3 * side
    diag_slot = 3 * side
    forward = 3 * (1 - core)
    free = 3 * core
    passed = 1 + core
    beside = 2 - core
    has_passed = inside(2 * core - 1)
    has_forward = inside(2 - 4 * core)
    from_partner = core == side

    def column(g, width):
        return pl.ds(pl.multiple_of(g * width, width), width)

    def remote(src, dst, sent, received, device):
        return pltpu.make_async_remote_copy(
            src_ref=src, dst_ref=dst, send_sem=sent, recv_sem=received,
            device_id=device, device_id_type=pl.DeviceIdType.MESH,
        )

    def near_copy(g, part, source, slot, kind, device):
        return remote(
            source.at[part], near.at[g, slot, part], near_send.at[g, kind, part], near_recv.at[g, slot, part], device
        )

    def partner_copy(g, part):
        return near_copy(g, part, kv.at[g], 3 * side, 0, partner)

    def beside_copy(g, part):
        return near_copy(g, part, kv.at[g], 1 + core, 1, sibling)

    def diag_copy(g, part):
        return near_copy(g, part, kv.at[g], 3 - 3 * side, 2, diagonal)

    def ahead_copy(g, part):
        return near_copy(g, part, near.at[g, partner_slot], diag_slot, 2, ahead)

    def relay_copy(g, part):
        return near_copy(g, part, near.at[g, forward], 2 - core, 3, sibling)

    def near_wait(g, part, slot):
        near_copy(g, part, near.at[g, slot], slot, 0, sibling).wait_recv()

    def grad_copy(g, part, slot, place, kind, device):
        return remote(
            gsend.at[g, slot, part], grecv.at[g, place, part],
            grad_send.at[g, kind, part], grad_recv.at[g, place, part], device,
        )

    def beside_grad(g, part):
        return grad_copy(g, part, beside, 0, 0, sibling)

    def passed_grad(g, part):
        return grad_copy(g, part, passed, 1, 1, sibling)

    def behind_grad(g, part):
        return grad_copy(g, part, diag_slot, 2, 2, behind)

    def partner_grad(g, part):
        return grad_copy(g, part, partner_slot, 3, 3, partner)

    def diag_grad(g, part):
        return grad_copy(g, part, diag_slot, 4, 2, diagonal)

    def kv_load(g, part):
        return pltpu.make_async_copy(
            kv_hbm.at[:, pl.ds(part * kv_width + g * HEAD, HEAD)], kv.at[g, part], kv_sem.at[g, part]
        )

    def load_copies(g):
        return (
            pltpu.make_async_copy(q_hbm.at[:, column(g, wide)], q.at[:, column(g, wide)], in_sem.at[g, 0]),
            pltpu.make_async_copy(do_hbm.at[:, column(g, wide)], do.at[:, column(g, wide)], in_sem.at[g, 1]),
        )

    barrier = pltpu.get_barrier_semaphore()

    def greet(device):
        pl.semaphore_signal(barrier, inc=1, device_id=device, device_id_type=pl.DeviceIdType.MESH)

    greet(partner)
    greet(sibling)

    @pl.when(has_ahead)
    def _():
        greet(ahead)

    @pl.when(has_behind)
    def _():
        greet(behind)

    for g in range(groups):
        for part in range(2):
            kv_load(g, part).start()
    for copy in load_copies(0):
        copy.start()
    for g in range(1, groups):
        for copy in load_copies(g):
            copy.start()

    for o in range(4):

        @pl.when(jnp.logical_not(exists(o)))
        def _():
            near[:, o] = jnp.zeros((groups, 2, rows, HEAD), near.dtype)

    @pl.when(jnp.logical_not(has_behind))
    def _():
        for g in range(groups):
            if g in GRAD_DIRECT:
                grecv[g, 4] = jnp.zeros((2, rows, HEAD), grecv.dtype)

    for g in range(groups):
        kv_load(g, 0).wait()
        kv_load(g, 1).wait()
    pl.semaphore_wait(barrier, 2 + has_ahead.astype(jnp.int32) + has_behind.astype(jnp.int32))

    for g in range(groups):
        for part in range(2):
            partner_copy(g, part).start()
        for part in range(2):
            beside_copy(g, part).start()

    own_block = slot_ref[me]
    live_count = count_ref[own_block]
    chosen = []
    bias = []
    for j in (1, 2):
        wanted = blocks_ref[j, own_block]
        hits = []
        for o in range(4):
            there = jnp.clip(me + OFFSETS[o], 0, n - 1)
            hits.append(exists(o) & (slot_ref[there] == wanted) & (live_count > j))
        chosen.append(hits)
        bias.append(jnp.where(hits[0] | hits[1] | hits[2] | hits[3], 0.0, NEG).astype(jnp.float32))

    def pick(g, part, hits):
        value = near[g, 0, part]
        for o in range(1, 4):
            value = jnp.where(hits[o], near[g, o, part], value)
        return value

    def from_diag(g):
        @pl.when(has_behind)
        def _():
            for part in range(2):
                near_wait(g, part, diag_slot)

                @pl.when(jnp.logical_not(from_partner))
                def _():
                    relay_copy(g, part).start()

    def plus(g, part, slot, place):
        both = gsend[g, slot, part].astype(jnp.float32) + grecv[g, place, part].astype(jnp.float32)
        gsend[g, slot, part] = both.astype(jnp.bfloat16)

    def combine(g):
        for part in range(2):

            @pl.when(has_forward)
            def _():
                passed_grad(g, part).wait_recv()
                plus(g, part, forward, 1)

            send_diag(g, part, jnp.logical_not(from_partner))
            send_partner(g, part, from_partner)

    def send_diag(g, part, mine):
        mine = jnp.logical_and(mine, has_behind)
        direct = among(g, GRAD_DIRECT)

        @pl.when(jnp.logical_and(mine, direct))
        def _():
            diag_grad(g, part).start()

        @pl.when(jnp.logical_and(mine, jnp.logical_not(direct)))
        def _():
            behind_grad(g, part).start()

    def send_partner(g, part, mine):
        direct = among(g, GRAD_DIRECT)

        @pl.when(jnp.logical_and(mine, jnp.logical_or(direct, jnp.logical_not(has_ahead))))
        def _():
            partner_grad(g, part).start()

    def add_ahead(g):
        @pl.when(jnp.logical_and(has_ahead, jnp.logical_not(among(g, GRAD_DIRECT))))
        def _():
            for part in range(2):
                grad_copy(g, part, 0, 2, 0, sibling).wait_recv()
                plus(g, part, partner_slot, 2)
                partner_grad(g, part).start()

    def at(index, pred, action):
        pl.when(pred)(functools.partial(action, index))

    others = pl.ds(rows, 2 * rows)

    def stacked(source, g, pair):
        starts = [pl.multiple_of(g * wide + (2 * pair + i) * HEAD, HEAD) for i in range(2)]
        return jnp.concatenate([source[:, pl.ds(s, HEAD)] for s in starts], axis=0)

    def weigh(g, pair, first, shifts):
        total = jnp.zeros((8, 2 * rows), jnp.float32)
        dot = jnp.zeros((8, 2 * rows), jnp.float32)
        height = rows // 2
        for j, shift in enumerate(shifts):
            for c in range(0, height, CHUNK):
                at_rows = pl.ds(first + j * height + c, CHUNK)
                weight = jnp.exp2(score[g, pair, at_rows] * (scale * LOG2E) - shift)
                score[g, pair, at_rows] = weight
                total = total + jnp.sum(weight.reshape(CHUNK // 8, 8, 2 * rows), axis=0)
                both = weight * pgrad[g, pair, at_rows]
                dot = dot + jnp.sum(both.reshape(CHUNK // 8, 8, 2 * rows), axis=0)
        return jnp.sum(total, axis=0, keepdims=True), jnp.sum(dot, axis=0, keepdims=True)

    def normalised(g, pair, part, factor):
        prob = score[g, pair, part] * stats[g, pair, factor : factor + 1]
        score_grads = prob * (pgrad[g, pair, part] - stats[g, pair, 5:6])
        return prob.astype(jnp.bfloat16), score_grads.astype(jnp.bfloat16)

    def products(g, pair, rounded, score_grads, key_grad, value_grad):
        return (
            key_grad + jnp.dot(score_grads, stacked(q, g, pair), preferred_element_type=jnp.float32),
            value_grad + jnp.dot(rounded, stacked(do, g, pair), preferred_element_type=jnp.float32),
        )

    def own_part(g, carry):
        for copy in load_copies(g):
            copy.wait()
        keys = kv[g, 0]
        values = kv[g, 1]
        for pair in range(pairs):
            raw = lax.dot_general(keys, stacked(q, g, pair), NT, preferred_element_type=jnp.float32)
            best = jnp.max(raw, axis=0, keepdims=True) * (scale * LOG2E)
            score[g, pair, pl.ds(0, rows)] = raw
            pgrad[g, pair, pl.ds(0, rows)] = lax.dot_general(
                values, stacked(do, g, pair), NT, preferred_element_type=jnp.float32
            )
            total, dot = weigh(g, pair, 0, [best] * 2)
            stats[g, pair, 0:1] = best
            stats[g, pair, 1:2] = total
            stats[g, pair, 2:3] = dot
        return carry

    def step(g, carry):
        for part in range(2):
            near_wait(g, part, beside)

        @pl.when(has_passed)
        def _():
            for part in range(2):
                near_wait(g, part, passed)

        for part in range(2):
            for j in range(2):
                picked[g, part, pl.ds(j * rows, rows)] = pick(g, part, chosen[j])
        keys = picked[g, 0]
        values = picked[g, 1]

        def matmuls(pair):
            raw = lax.dot_general(keys, stacked(q, g, pair), NT, preferred_element_type=jnp.float32)
            best = stats[g, pair, 0:1]
            for j in range(2):
                top = jnp.max(raw[j * rows : (j + 1) * rows], axis=0, keepdims=True) * (scale * LOG2E)
                best = jnp.maximum(best, top + bias[j])
            score[g, pair, others] = raw
            pgrad[g, pair, others] = lax.dot_general(
                values, stacked(do, g, pair), NT, preferred_element_type=jnp.float32
            )
            return best

        def softmax(pair, best):
            factor = jnp.exp2(stats[g, pair, 0:1] - best)
            shifts = [best - bias[j // 2] for j in range(4)]
            total, dot = weigh(g, pair, rows, shifts)
            inverse = 1.0 / (total + stats[g, pair, 1:2] * factor)
            delta = (dot + stats[g, pair, 2:3] * factor) * inverse
            stats[g, pair, 3:4] = inverse * factor
            stats[g, pair, 4:5] = inverse
            stats[g, pair, 5:6] = delta

        def sums(pair, key_grad, value_grad):
            return products(g, pair, *normalised(g, pair, others, 4), key_grad, value_grad)

        key_grad = jnp.zeros((2 * rows, HEAD), jnp.float32)
        value_grad = jnp.zeros((2 * rows, HEAD), jnp.float32)
        best0 = matmuls(0)
        best1 = matmuls(1)
        softmax(0, best0)
        best2 = matmuls(2)
        key_grad, value_grad = sums(0, key_grad, value_grad)
        softmax(1, best1)
        at(g - 1, g > 0, combine)
        at(g + 1, g + 1 < groups, from_diag)
        best3 = matmuls(3)
        key_grad, value_grad = sums(1, key_grad, value_grad)
        softmax(2, best2)
        key_grad, value_grad = sums(2, key_grad, value_grad)
        softmax(3, best3)
        key_grad, value_grad = sums(3, key_grad, value_grad)
        for part, grad in ((0, key_grad * scale), (1, value_grad)):
            first = grad[:rows].astype(jnp.bfloat16)
            second = grad[rows:].astype(jnp.bfloat16)
            nothing = jnp.zeros_like(first)
            for o in range(4):
                gsend[g, o, part] = jnp.where(chosen[0][o], first, jnp.where(chosen[1][o], second, nothing))

        for part in range(2):

            @pl.when(has_passed)
            def _():
                passed_grad(g, part).start()

            send_diag(g, part, from_partner)
            send_partner(g, part, jnp.logical_not(from_partner))
        for part in range(2):
            beside_grad(g, part).start()
        return carry

    def results(g, carry):
        keys_t = jnp.concatenate([kv[g, 0], picked[g, 0]], axis=0).T
        values_t = jnp.concatenate([kv[g, 1], picked[g, 1]], axis=0).T
        key_grad = jnp.zeros((rows, HEAD), jnp.float32)
        value_grad = jnp.zeros((rows, HEAD), jnp.float32)
        for pair in range(pairs):
            own_rounded, own_grads = normalised(g, pair, pl.ds(0, rows), 3)
            rounded, score_grads = normalised(g, pair, others, 4)
            key_grad, value_grad = products(g, pair, own_rounded, own_grads, key_grad, value_grad)
            rounded = jnp.concatenate([own_rounded, rounded], axis=0)
            score_grads = jnp.concatenate([own_grads, score_grads], axis=0)
            mixed = jnp.dot(values_t, rounded, preferred_element_type=jnp.float32)
            query_grad = jnp.dot(keys_t, score_grads, preferred_element_type=jnp.float32) * scale
            mixed = mixed.astype(jnp.bfloat16).T
            query_grad = query_grad.astype(jnp.bfloat16).T
            for i in range(2):
                where = pl.ds(pl.multiple_of(g * wide + (2 * pair + i) * HEAD, HEAD), HEAD)
                att[:, where] = mixed[i * rows : (i + 1) * rows]
                dq[:, where] = query_grad[i * rows : (i + 1) * rows]
        own_grad[g, 0] = key_grad * scale
        own_grad[g, 1] = value_grad
        at(groups - 1, g == 0, combine)
        at(g + 1, g + 2 < groups, add_ahead)
        return carry

    lax.fori_loop(0, groups, own_part, 0)

    for g in range(groups):
        for part in range(2):
            near_wait(g, part, partner_slot)
            if g not in KV_DIRECT:

                @pl.when(has_ahead)
                def _():
                    ahead_copy(g, part).start()

            @pl.when(from_partner)
            def _():
                relay_copy(g, part).start()

        if g == 0:

            @pl.when(has_behind)
            def _():
                for h in KV_DIRECT:
                    for part in range(2):
                        diag_copy(h, part).start()

    from_diag(0)
    lax.fori_loop(0, groups, step, 0)
    add_ahead(0)
    lax.fori_loop(0, groups, results, 0)
    def finish(g, carry):
        direct = among(g, GRAD_DIRECT)
        for part in range(2):
            beside_grad(g, part).wait_recv()
            total = own_grad[g, part] + grecv[g, 0, part].astype(jnp.float32)
            where = pl.ds(pl.multiple_of(part * kv_width + g * HEAD, HEAD), HEAD)

            @pl.when(jnp.logical_and(direct, has_behind))
            def _():
                grad_copy(g, part, 0, 4, 0, partner).wait_recv()

            grad_copy(g, part, 0, 3, 0, partner).wait_recv()
            total = total + grecv[g, 3, part].astype(jnp.float32)

            @pl.when(direct)
            def _():
                kvg[:, where] = (total + grecv[g, 4, part].astype(jnp.float32)).astype(jnp.bfloat16)

            @pl.when(jnp.logical_not(direct))
            def _():
                kvg[:, where] = total.astype(jnp.bfloat16)

        return carry

    def drain_near(g, carry):
        direct = among(g, KV_DIRECT)
        for part in range(2):
            partner_copy(g, part).wait_send()
            beside_copy(g, part).wait_send()

            @pl.when(jnp.logical_and(direct, has_behind))
            def _():
                diag_copy(g, part).wait_send()

            @pl.when(jnp.logical_and(jnp.logical_not(direct), has_ahead))
            def _():
                ahead_copy(g, part).wait_send()

            @pl.when(has_forward)
            def _():
                relay_copy(g, part).wait_send()

        return carry

    def drain_grads(g, carry):
        for part in range(2):
            beside_grad(g, part).wait_send()
            partner_grad(g, part).wait_send()

            @pl.when(has_passed)
            def _():
                passed_grad(g, part).wait_send()

            @pl.when(has_behind)
            def _():
                behind_grad(g, part).wait_send()

        return carry

    lax.fori_loop(0, groups, drain_near, 0)
    lax.fori_loop(0, groups - 2, finish, 0)
    add_ahead(groups - 1)
    lax.fori_loop(0, groups - 2, drain_grads, 0)
    lax.fori_loop(groups - 2, groups, finish, 0)
    lax.fori_loop(groups - 2, groups, drain_grads, 0)


def flush(att, dq, kvg, att_out, dq_out, kvg_out, out_sem):
    width = kvg.shape[1]
    pieces = [(kvg, kvg_out, 0)]
    for start in range(0, att.shape[1], width):
        pieces.append((att, att_out, start))
        pieces.append((dq, dq_out, start))
    stores = []
    for i, (source, result, start) in enumerate(pieces):
        part = pl.ds(start, width)
        stores.append(pltpu.make_async_copy(source.at[:, part], result.at[:, part], out_sem.at[i]))
    for store in stores:
        store.start()
    for store in stores:
        store.wait()


def body(queries, keys_values, out_grad, key_blocks, key_count, block_at_slot):
    n = lax.axis_size("ctx")
    rows, width = queries.shape
    kv_width = keys_values.shape[1] // 2
    groups = kv_width // HEAD
    repeats = width // kv_width
    scalars = pl.BlockSpec(memory_space=pltpu.SMEM)
    wide = pltpu.VMEM((rows, width), jnp.bfloat16)
    narrow = pltpu.VMEM((rows, 2 * kv_width), jnp.bfloat16)
    dma = pltpu.SemaphoreType.DMA
    shapes = (
        jax.ShapeDtypeStruct((rows, width), jnp.bfloat16),
        jax.ShapeDtypeStruct((rows, width), jnp.bfloat16),
        jax.ShapeDtypeStruct((rows, 2 * kv_width), jnp.bfloat16),
    )

    def blocks(*lead, dtype=jnp.bfloat16):
        return pltpu.VMEM((*lead, rows, HEAD), dtype)

    pieces = 2 * (width // (2 * kv_width)) + 1
    held = pl.BlockSpec(memory_space=pltpu.VMEM)
    pair_float = pltpu.VMEM((groups, repeats // 2, 3 * rows, 2 * rows), jnp.float32)
    pair_stats = pltpu.VMEM((groups, repeats // 2, 8, 2 * rows), jnp.float32)
    results = pl.pallas_call(
        functools.partial(kernel, n, groups, repeats),
        out_shape=(wide, wide, narrow),
        in_specs=[scalars] * 3 + [pl.BlockSpec(memory_space=pltpu.HBM)] * 3,
        out_specs=(held, held, held),
        scratch_shapes=[
            wide, blocks(groups, 2), wide, blocks(groups, 4, 2),
            pltpu.VMEM((groups, 2, 2 * rows, HEAD), jnp.bfloat16), pair_float, pair_float, pair_stats,
            blocks(groups, 2, dtype=jnp.float32), blocks(groups, 4, 2), blocks(groups, 5, 2),
            dma((groups, 2)), dma((groups, 2)),
            dma((groups, 4, 2)), dma((groups, 4, 2)), dma((groups, 4, 2)), dma((groups, 5, 2)),
        ],
        compiler_params=pltpu.CompilerParams(
            collective_id=0, has_side_effects=True, vmem_limit_bytes=61 * 1024 * 1024
        ),
    )(key_blocks.T, key_count, block_at_slot, queries, keys_values, out_grad)
    return pl.pallas_call(
        flush,
        out_shape=shapes,
        in_specs=[held] * 3,
        out_specs=(pl.BlockSpec(memory_space=pltpu.HBM),) * 3,
        scratch_shapes=[dma((pieces,))],
        compiler_params=pltpu.CompilerParams(vmem_limit_bytes=16 * 1024 * 1024),
    )(*results)


def solution(mesh):
    sharded = P(("groups", "ctx"), None)
    return jax.shard_map(
        body,
        mesh=mesh,
        in_specs=(sharded, sharded, sharded, P("groups", None), P("groups"), P("groups")),
        out_specs=(sharded, sharded, sharded),
        check_vma=False,
    )
```

```python
import functools

import jax
import jax.numpy as jnp
from jax import lax
from jax.experimental import pallas as pl
from jax.experimental.pallas import tpu as pltpu
from jax.sharding import PartitionSpec as P

HEAD = 128
OFFSETS = (-2, -1, 1, 2)
LOG2E = 1.4426950408889634
NEG = -1e30
NT = (((1,), (1,)), ((), ()))
KV_DIRECT = ()
GRAD_DIRECT = (0, 1, 3, 5, 7)
CHUNK = 32


def among(g, members):
    if isinstance(g, int):
        return g in members
    found = jnp.bool_(False)
    for m in members:
        found = jnp.logical_or(found, g == m)
    return found


def kernel(
    n, groups, repeats,
    blocks_ref, count_ref, slot_ref, q_hbm, kv_hbm, do_hbm,
    att, dq, kvg,
    q, kv, do, near, picked, score, pgrad, stats, own_grad, gsend, grecv,
    in_sem, kv_sem, near_send, near_recv, grad_send, grad_recv,
):
    rows = q.shape[0]
    wide = repeats * HEAD
    kv_width = groups * HEAD
    pairs = repeats // 2
    scale = HEAD ** (-0.5)
    me = lax.axis_index("ctx")
    core = lax.rem(me, 2)
    side = lax.rem(me // 2, 2)
    along = 4 - 8 * side

    def inside(d):
        return jnp.logical_and(me + d >= 0, me + d < n)

    def exists(o):
        return inside(OFFSETS[o])

    sibling = {"ctx": me + 1 - 2 * core}
    partner = {"ctx": me + 2 - 4 * side}
    diagonal = {"ctx": me - 2 + 4 * side}
    ahead = {"ctx": me + along}
    behind = {"ctx": me - along}
    has_ahead = inside(along)
    has_behind = inside(-along)
    partner_slot = 3 - 3 * side
    diag_slot = 3 * side
    forward = 3 * (1 - core)
    free = 3 * core
    passed = 1 + core
    beside = 2 - core
    has_passed = inside(2 * core - 1)
    has_forward = inside(2 - 4 * core)
    from_partner = core == side

    def column(g, width):
        return pl.ds(pl.multiple_of(g * width, width), width)

    def remote(src, dst, sent, received, device):
        return pltpu.make_async_remote_copy(
            src_ref=src, dst_ref=dst, send_sem=sent, recv_sem=received,
            device_id=device, device_id_type=pl.DeviceIdType.MESH,
        )

    def near_copy(g, part, source, slot, kind, device):
        return remote(
            source.at[part], near.at[g, slot, part], near_send.at[g, kind, part], near_recv.at[g, slot, part], device
        )

    def partner_copy(g, part):
        return near_copy(g, part, kv.at[g], 3 * side, 0, partner)

    def beside_copy(g, part):
        return near_copy(g, part, kv.at[g], 1 + core, 1, sibling)

    def diag_copy(g, part):
        return near_copy(g, part, kv.at[g], 3 - 3 * side, 2, diagonal)

    def ahead_copy(g, part):
        return near_copy(g, part, near.at[g, partner_slot], diag_slot, 2, ahead)

    def relay_copy(g, part):
        return near_copy(g, part, near.at[g, forward], 2 - core, 3, sibling)

    def near_wait(g, part, slot):
        near_copy(g, part, near.at[g, slot], slot, 0, sibling).wait_recv()

    def grad_copy(g, part, slot, place, kind, device):
        return remote(
            gsend.at[g, slot, part], grecv.at[g, place, part],
            grad_send.at[g, kind, part], grad_recv.at[g, place, part], device,
        )

    def beside_grad(g, part):
        return grad_copy(g, part, beside, 0, 0, sibling)

    def passed_grad(g, part):
        return grad_copy(g, part, passed, 1, 1, sibling)

    def behind_grad(g, part):
        return grad_copy(g, part, diag_slot, 2, 2, behind)

    def partner_grad(g, part):
        return grad_copy(g, part, partner_slot, 3, 3, partner)

    def diag_grad(g, part):
        return grad_copy(g, part, diag_slot, 4, 2, diagonal)

    def kv_load(g, part):
        return pltpu.make_async_copy(
            kv_hbm.at[:, pl.ds(part * kv_width + g * HEAD, HEAD)], kv.at[g, part], kv_sem.at[g, part]
        )

    def load_copies(g):
        return (
            pltpu.make_async_copy(q_hbm.at[:, column(g, wide)], q.at[:, column(g, wide)], in_sem.at[g, 0]),
            pltpu.make_async_copy(do_hbm.at[:, column(g, wide)], do.at[:, column(g, wide)], in_sem.at[g, 1]),
        )

    barrier = pltpu.get_barrier_semaphore()

    def greet(device):
        pl.semaphore_signal(barrier, inc=1, device_id=device, device_id_type=pl.DeviceIdType.MESH)

    greet(partner)
    greet(sibling)

    @pl.when(has_ahead)
    def _():
        greet(ahead)

    @pl.when(has_behind)
    def _():
        greet(behind)

    for g in range(groups):
        for part in range(2):
            kv_load(g, part).start()
    for copy in load_copies(0):
        copy.start()
    for g in range(1, groups):
        for copy in load_copies(g):
            copy.start()

    for o in range(4):

        @pl.when(jnp.logical_not(exists(o)))
        def _():
            near[:, o] = jnp.zeros((groups, 2, rows, HEAD), near.dtype)

    @pl.when(jnp.logical_not(has_behind))
    def _():
        for g in range(groups):
            for part in range(2):
                if 2 * g + part in GRAD_DIRECT:
                    grecv[g, 4, part] = jnp.zeros((rows, HEAD), grecv.dtype)

    for g in range(groups):
        kv_load(g, 0).wait()
        kv_load(g, 1).wait()
    pl.semaphore_wait(barrier, 2 + has_ahead.astype(jnp.int32) + has_behind.astype(jnp.int32))

    for g in range(groups):
        for part in range(2):
            partner_copy(g, part).start()
        for part in range(2):
            beside_copy(g, part).start()

    own_block = slot_ref[me]
    live_count = count_ref[own_block]
    chosen = []
    bias = []
    for j in (1, 2):
        wanted = blocks_ref[j, own_block]
        hits = []
        for o in range(4):
            there = jnp.clip(me + OFFSETS[o], 0, n - 1)
            hits.append(exists(o) & (slot_ref[there] == wanted) & (live_count > j))
        chosen.append(hits)
        bias.append(jnp.where(hits[0] | hits[1] | hits[2] | hits[3], 0.0, NEG).astype(jnp.float32))

    def pick(g, part, hits):
        value = near[g, 0, part]
        for o in range(1, 4):
            value = jnp.where(hits[o], near[g, o, part], value)
        return value

    def from_diag(g):
        @pl.when(has_behind)
        def _():
            for part in range(2):
                near_wait(g, part, diag_slot)

                @pl.when(jnp.logical_not(from_partner))
                def _():
                    relay_copy(g, part).start()

    def plus(g, part, slot, place):
        both = gsend[g, slot, part].astype(jnp.float32) + grecv[g, place, part].astype(jnp.float32)
        gsend[g, slot, part] = both.astype(jnp.bfloat16)

    def combine(g):
        for part in range(2):

            @pl.when(has_forward)
            def _():
                passed_grad(g, part).wait_recv()
                plus(g, part, forward, 1)

            send_diag(g, part, jnp.logical_not(from_partner))
            send_partner(g, part, from_partner)

    def send_diag(g, part, mine):
        mine = jnp.logical_and(mine, has_behind)
        direct = among(2 * g + part, GRAD_DIRECT)

        @pl.when(jnp.logical_and(mine, direct))
        def _():
            diag_grad(g, part).start()

        @pl.when(jnp.logical_and(mine, jnp.logical_not(direct)))
        def _():
            behind_grad(g, part).start()

    def send_partner(g, part, mine):
        direct = among(2 * g + part, GRAD_DIRECT)

        @pl.when(jnp.logical_and(mine, jnp.logical_or(direct, jnp.logical_not(has_ahead))))
        def _():
            partner_grad(g, part).start()

    def add_ahead(g):
        for part in range(2):

            @pl.when(jnp.logical_and(has_ahead, jnp.logical_not(among(2 * g + part, GRAD_DIRECT))))
            def _():
                grad_copy(g, part, 0, 2, 0, sibling).wait_recv()
                plus(g, part, partner_slot, 2)
                partner_grad(g, part).start()

    def at(index, pred, action):
        pl.when(pred)(functools.partial(action, index))

    others = pl.ds(rows, 2 * rows)

    def stacked(source, g, pair):
        starts = [pl.multiple_of(g * wide + (2 * pair + i) * HEAD, HEAD) for i in range(2)]
        return jnp.concatenate([source[:, pl.ds(s, HEAD)] for s in starts], axis=0)

    def weigh(g, pair, first, shifts):
        total = jnp.zeros((8, 2 * rows), jnp.float32)
        dot = jnp.zeros((8, 2 * rows), jnp.float32)
        height = rows // 2
        for j, shift in enumerate(shifts):
            for c in range(0, height, CHUNK):
                at_rows = pl.ds(first + j * height + c, CHUNK)
                weight = jnp.exp2(score[g, pair, at_rows] * (scale * LOG2E) - shift)
                score[g, pair, at_rows] = weight
                total = total + jnp.sum(weight.reshape(CHUNK // 8, 8, 2 * rows), axis=0)
                both = weight * pgrad[g, pair, at_rows]
                dot = dot + jnp.sum(both.reshape(CHUNK // 8, 8, 2 * rows), axis=0)
        return jnp.sum(total, axis=0, keepdims=True), jnp.sum(dot, axis=0, keepdims=True)

    def normalised(g, pair, part, factor):
        prob = score[g, pair, part] * stats[g, pair, factor : factor + 1]
        score_grads = prob * (pgrad[g, pair, part] - stats[g, pair, 5:6])
        return prob.astype(jnp.bfloat16), score_grads.astype(jnp.bfloat16)

    def products(g, pair, rounded, score_grads, key_grad, value_grad):
        return (
            key_grad + jnp.dot(score_grads, stacked(q, g, pair), preferred_element_type=jnp.float32),
            value_grad + jnp.dot(rounded, stacked(do, g, pair), preferred_element_type=jnp.float32),
        )

    def own_part(g, carry):
        for copy in load_copies(g):
            copy.wait()
        keys = kv[g, 0]
        values = kv[g, 1]
        for pair in range(pairs):
            raw = lax.dot_general(keys, stacked(q, g, pair), NT, preferred_element_type=jnp.float32)
            best = jnp.max(raw, axis=0, keepdims=True) * (scale * LOG2E)
            score[g, pair, pl.ds(0, rows)] = raw
            pgrad[g, pair, pl.ds(0, rows)] = lax.dot_general(
                values, stacked(do, g, pair), NT, preferred_element_type=jnp.float32
            )
            total, dot = weigh(g, pair, 0, [best] * 2)
            stats[g, pair, 0:1] = best
            stats[g, pair, 1:2] = total
            stats[g, pair, 2:3] = dot
        return carry

    def step(g, carry):
        for part in range(2):
            near_wait(g, part, beside)

        @pl.when(has_passed)
        def _():
            for part in range(2):
                near_wait(g, part, passed)

        for part in range(2):
            for j in range(2):
                picked[g, part, pl.ds(j * rows, rows)] = pick(g, part, chosen[j])
        keys = picked[g, 0]
        values = picked[g, 1]

        def matmuls(pair):
            raw = lax.dot_general(keys, stacked(q, g, pair), NT, preferred_element_type=jnp.float32)
            best = stats[g, pair, 0:1]
            for j in range(2):
                top = jnp.max(raw[j * rows : (j + 1) * rows], axis=0, keepdims=True) * (scale * LOG2E)
                best = jnp.maximum(best, top + bias[j])
            score[g, pair, others] = raw
            pgrad[g, pair, others] = lax.dot_general(
                values, stacked(do, g, pair), NT, preferred_element_type=jnp.float32
            )
            return best

        def softmax(pair, best):
            factor = jnp.exp2(stats[g, pair, 0:1] - best)
            shifts = [best - bias[j // 2] for j in range(4)]
            total, dot = weigh(g, pair, rows, shifts)
            inverse = 1.0 / (total + stats[g, pair, 1:2] * factor)
            delta = (dot + stats[g, pair, 2:3] * factor) * inverse
            stats[g, pair, 3:4] = inverse * factor
            stats[g, pair, 4:5] = inverse
            stats[g, pair, 5:6] = delta

        def sums(pair, key_grad, value_grad):
            return products(g, pair, *normalised(g, pair, others, 4), key_grad, value_grad)

        key_grad = jnp.zeros((2 * rows, HEAD), jnp.float32)
        value_grad = jnp.zeros((2 * rows, HEAD), jnp.float32)
        best0 = matmuls(0)
        best1 = matmuls(1)
        softmax(0, best0)
        best2 = matmuls(2)
        key_grad, value_grad = sums(0, key_grad, value_grad)
        softmax(1, best1)
        at(g - 1, g > 0, combine)
        at(g + 1, g + 1 < groups, from_diag)
        best3 = matmuls(3)
        key_grad, value_grad = sums(1, key_grad, value_grad)
        softmax(2, best2)
        key_grad, value_grad = sums(2, key_grad, value_grad)
        softmax(3, best3)
        key_grad, value_grad = sums(3, key_grad, value_grad)
        for part, grad in ((0, key_grad * scale), (1, value_grad)):
            first = grad[:rows].astype(jnp.bfloat16)
            second = grad[rows:].astype(jnp.bfloat16)
            nothing = jnp.zeros_like(first)
            for o in range(4):
                gsend[g, o, part] = jnp.where(chosen[0][o], first, jnp.where(chosen[1][o], second, nothing))

        for part in range(2):

            @pl.when(has_passed)
            def _():
                passed_grad(g, part).start()

            send_diag(g, part, from_partner)
            send_partner(g, part, jnp.logical_not(from_partner))
        for part in range(2):
            beside_grad(g, part).start()
        return carry

    def results(g, carry):
        keys_t = jnp.concatenate([kv[g, 0], picked[g, 0]], axis=0).T
        values_t = jnp.concatenate([kv[g, 1], picked[g, 1]], axis=0).T
        key_grad = jnp.zeros((rows, HEAD), jnp.float32)
        value_grad = jnp.zeros((rows, HEAD), jnp.float32)
        for pair in range(pairs):
            own_rounded, own_grads = normalised(g, pair, pl.ds(0, rows), 3)
            rounded, score_grads = normalised(g, pair, others, 4)
            key_grad, value_grad = products(g, pair, own_rounded, own_grads, key_grad, value_grad)
            rounded = jnp.concatenate([own_rounded, rounded], axis=0)
            score_grads = jnp.concatenate([own_grads, score_grads], axis=0)
            mixed = jnp.dot(values_t, rounded, preferred_element_type=jnp.float32)
            query_grad = jnp.dot(keys_t, score_grads, preferred_element_type=jnp.float32) * scale
            mixed = mixed.astype(jnp.bfloat16).T
            query_grad = query_grad.astype(jnp.bfloat16).T
            for i in range(2):
                where = pl.ds(pl.multiple_of(g * wide + (2 * pair + i) * HEAD, HEAD), HEAD)
                att[:, where] = mixed[i * rows : (i + 1) * rows]
                dq[:, where] = query_grad[i * rows : (i + 1) * rows]
        own_grad[g, 0] = key_grad * scale
        own_grad[g, 1] = value_grad
        at(groups - 1, g == 0, combine)
        at(g + 1, g + 2 < groups, add_ahead)
        return carry

    lax.fori_loop(0, groups, own_part, 0)

    for g in range(groups):
        for part in range(2):
            near_wait(g, part, partner_slot)
            if g not in KV_DIRECT:

                @pl.when(has_ahead)
                def _():
                    ahead_copy(g, part).start()

            @pl.when(from_partner)
            def _():
                relay_copy(g, part).start()

        if g == 0:

            @pl.when(has_behind)
            def _():
                for h in KV_DIRECT:
                    for part in range(2):
                        diag_copy(h, part).start()

    from_diag(0)
    lax.fori_loop(0, groups, step, 0)
    add_ahead(0)
    lax.fori_loop(0, groups, results, 0)
    def finish(g, carry):
        for part in range(2):
            direct = among(2 * g + part, GRAD_DIRECT)
            beside_grad(g, part).wait_recv()
            total = own_grad[g, part] + grecv[g, 0, part].astype(jnp.float32)
            where = pl.ds(pl.multiple_of(part * kv_width + g * HEAD, HEAD), HEAD)

            @pl.when(jnp.logical_and(direct, has_behind))
            def _():
                grad_copy(g, part, 0, 4, 0, partner).wait_recv()

            grad_copy(g, part, 0, 3, 0, partner).wait_recv()
            total = total + grecv[g, 3, part].astype(jnp.float32)

            @pl.when(direct)
            def _():
                kvg[:, where] = (total + grecv[g, 4, part].astype(jnp.float32)).astype(jnp.bfloat16)

            @pl.when(jnp.logical_not(direct))
            def _():
                kvg[:, where] = total.astype(jnp.bfloat16)

        return carry

    def drain_near(g, carry):
        direct = among(g, KV_DIRECT)
        for part in range(2):
            partner_copy(g, part).wait_send()
            beside_copy(g, part).wait_send()

            @pl.when(jnp.logical_and(direct, has_behind))
            def _():
                diag_copy(g, part).wait_send()

            @pl.when(jnp.logical_and(jnp.logical_not(direct), has_ahead))
            def _():
                ahead_copy(g, part).wait_send()

            @pl.when(has_forward)
            def _():
                relay_copy(g, part).wait_send()

        return carry

    def drain_grads(g, carry):
        for part in range(2):
            beside_grad(g, part).wait_send()
            partner_grad(g, part).wait_send()

            @pl.when(has_passed)
            def _():
                passed_grad(g, part).wait_send()

            @pl.when(has_behind)
            def _():
                behind_grad(g, part).wait_send()

        return carry

    lax.fori_loop(0, groups, drain_near, 0)
    add_ahead(groups - 1)
    lax.fori_loop(0, groups, finish, 0)
    lax.fori_loop(0, groups, drain_grads, 0)


def flush(att, dq, kvg, att_out, dq_out, kvg_out, out_sem):
    width = kvg.shape[1]
    pieces = [(kvg, kvg_out, 0)]
    for start in range(0, att.shape[1], width):
        pieces.append((att, att_out, start))
        pieces.append((dq, dq_out, start))
    stores = []
    for i, (source, result, start) in enumerate(pieces):
        part = pl.ds(start, width)
        stores.append(pltpu.make_async_copy(source.at[:, part], result.at[:, part], out_sem.at[i]))
    for store in stores:
        store.start()
    for store in stores:
        store.wait()


def body(queries, keys_values, out_grad, key_blocks, key_count, block_at_slot):
    n = lax.axis_size("ctx")
    rows, width = queries.shape
    kv_width = keys_values.shape[1] // 2
    groups = kv_width // HEAD
    repeats = width // kv_width
    scalars = pl.BlockSpec(memory_space=pltpu.SMEM)
    wide = pltpu.VMEM((rows, width), jnp.bfloat16)
    narrow = pltpu.VMEM((rows, 2 * kv_width), jnp.bfloat16)
    dma = pltpu.SemaphoreType.DMA
    shapes = (
        jax.ShapeDtypeStruct((rows, width), jnp.bfloat16),
        jax.ShapeDtypeStruct((rows, width), jnp.bfloat16),
        jax.ShapeDtypeStruct((rows, 2 * kv_width), jnp.bfloat16),
    )

    def blocks(*lead, dtype=jnp.bfloat16):
        return pltpu.VMEM((*lead, rows, HEAD), dtype)

    pieces = 2 * (width // (2 * kv_width)) + 1
    held = pl.BlockSpec(memory_space=pltpu.VMEM)
    pair_float = pltpu.VMEM((groups, repeats // 2, 3 * rows, 2 * rows), jnp.float32)
    pair_stats = pltpu.VMEM((groups, repeats // 2, 8, 2 * rows), jnp.float32)
    results = pl.pallas_call(
        functools.partial(kernel, n, groups, repeats),
        out_shape=(wide, wide, narrow),
        in_specs=[scalars] * 3 + [pl.BlockSpec(memory_space=pltpu.HBM)] * 3,
        out_specs=(held, held, held),
        scratch_shapes=[
            wide, blocks(groups, 2), wide, blocks(groups, 4, 2),
            pltpu.VMEM((groups, 2, 2 * rows, HEAD), jnp.bfloat16), pair_float, pair_float, pair_stats,
            blocks(groups, 2, dtype=jnp.float32), blocks(groups, 4, 2), blocks(groups, 5, 2),
            dma((groups, 2)), dma((groups, 2)),
            dma((groups, 4, 2)), dma((groups, 4, 2)), dma((groups, 4, 2)), dma((groups, 5, 2)),
        ],
        compiler_params=pltpu.CompilerParams(
            collective_id=0, has_side_effects=True, vmem_limit_bytes=61 * 1024 * 1024
        ),
    )(key_blocks.T, key_count, block_at_slot, queries, keys_values, out_grad)
    return pl.pallas_call(
        flush,
        out_shape=shapes,
        in_specs=[held] * 3,
        out_specs=(pl.BlockSpec(memory_space=pltpu.HBM),) * 3,
        scratch_shapes=[dma((pieces,))],
        compiler_params=pltpu.CompilerParams(vmem_limit_bytes=16 * 1024 * 1024),
    )(*results)


def solution(mesh):
    sharded = P(("groups", "ctx"), None)
    return jax.shard_map(
        body,
        mesh=mesh,
        in_specs=(sharded, sharded, sharded, P("groups", None), P("groups"), P("groups")),
        out_specs=(sharded, sharded, sharded),
        check_vma=False,
    )
```

```python
import functools

import jax
import jax.numpy as jnp
from jax import lax
from jax.experimental import pallas as pl
from jax.experimental.pallas import tpu as pltpu
from jax.sharding import PartitionSpec as P

HEAD = 128
OFFSETS = (-2, -1, 1, 2)
LOG2E = 1.4426950408889634
NEG = -1e30
NT = (((1,), (1,)), ((), ()))
KV_DIRECT = ()
GRAD_DIRECT = (0, 1, 3, 5, 7)
CHUNK = 64


def among(g, members):
    if isinstance(g, int):
        return g in members
    found = jnp.bool_(False)
    for m in members:
        found = jnp.logical_or(found, g == m)
    return found


def kernel(
    n, groups, repeats,
    blocks_ref, count_ref, slot_ref, q_hbm, kv_hbm, do_hbm,
    att, dq, kvg,
    q, kv, do, near, picked, score, pgrad, stats, own_grad, gsend, grecv,
    in_sem, kv_sem, near_send, near_recv, grad_send, grad_recv,
):
    rows = q.shape[0]
    wide = repeats * HEAD
    kv_width = groups * HEAD
    pairs = repeats // 2
    scale = HEAD ** (-0.5)
    me = lax.axis_index("ctx")
    core = lax.rem(me, 2)
    side = lax.rem(me // 2, 2)
    along = 4 - 8 * side

    def inside(d):
        return jnp.logical_and(me + d >= 0, me + d < n)

    def exists(o):
        return inside(OFFSETS[o])

    sibling = {"ctx": me + 1 - 2 * core}
    partner = {"ctx": me + 2 - 4 * side}
    diagonal = {"ctx": me - 2 + 4 * side}
    ahead = {"ctx": me + along}
    behind = {"ctx": me - along}
    has_ahead = inside(along)
    has_behind = inside(-along)
    partner_slot = 3 - 3 * side
    diag_slot = 3 * side
    forward = 3 * (1 - core)
    free = 3 * core
    passed = 1 + core
    beside = 2 - core
    has_passed = inside(2 * core - 1)
    has_forward = inside(2 - 4 * core)
    from_partner = core == side

    def column(g, width):
        return pl.ds(pl.multiple_of(g * width, width), width)

    def remote(src, dst, sent, received, device):
        return pltpu.make_async_remote_copy(
            src_ref=src, dst_ref=dst, send_sem=sent, recv_sem=received,
            device_id=device, device_id_type=pl.DeviceIdType.MESH,
        )

    def near_copy(g, part, source, slot, kind, device):
        return remote(
            source.at[part], near.at[g, slot, part], near_send.at[g, kind, part], near_recv.at[g, slot, part], device
        )

    def partner_copy(g, part):
        return near_copy(g, part, kv.at[g], 3 * side, 0, partner)

    def beside_copy(g, part):
        return near_copy(g, part, kv.at[g], 1 + core, 1, sibling)

    def diag_copy(g, part):
        return near_copy(g, part, kv.at[g], 3 - 3 * side, 2, diagonal)

    def ahead_copy(g, part):
        return near_copy(g, part, near.at[g, partner_slot], diag_slot, 2, ahead)

    def relay_copy(g, part):
        return near_copy(g, part, near.at[g, forward], 2 - core, 3, sibling)

    def near_wait(g, part, slot):
        near_copy(g, part, near.at[g, slot], slot, 0, sibling).wait_recv()

    def grad_copy(g, part, slot, place, kind, device):
        return remote(
            gsend.at[g, slot, part], grecv.at[g, place, part],
            grad_send.at[g, kind, part], grad_recv.at[g, place, part], device,
        )

    def beside_grad(g, part):
        return grad_copy(g, part, beside, 0, 0, sibling)

    def passed_grad(g, part):
        return grad_copy(g, part, passed, 1, 1, sibling)

    def behind_grad(g, part):
        return grad_copy(g, part, diag_slot, 2, 2, behind)

    def partner_grad(g, part):
        return grad_copy(g, part, partner_slot, 3, 3, partner)

    def diag_grad(g, part):
        return grad_copy(g, part, diag_slot, 4, 2, diagonal)

    def kv_load(g, part):
        return pltpu.make_async_copy(
            kv_hbm.at[:, pl.ds(part * kv_width + g * HEAD, HEAD)], kv.at[g, part], kv_sem.at[g, part]
        )

    def load_copies(g):
        return (
            pltpu.make_async_copy(q_hbm.at[:, column(g, wide)], q.at[:, column(g, wide)], in_sem.at[g, 0]),
            pltpu.make_async_copy(do_hbm.at[:, column(g, wide)], do.at[:, column(g, wide)], in_sem.at[g, 1]),
        )

    barrier = pltpu.get_barrier_semaphore()

    def greet(device):
        pl.semaphore_signal(barrier, inc=1, device_id=device, device_id_type=pl.DeviceIdType.MESH)

    greet(partner)
    greet(sibling)

    @pl.when(has_ahead)
    def _():
        greet(ahead)

    @pl.when(has_behind)
    def _():
        greet(behind)

    for g in range(groups):
        for part in range(2):
            kv_load(g, part).start()
    for copy in load_copies(0):
        copy.start()
    for g in range(1, groups):
        for copy in load_copies(g):
            copy.start()

    for o in range(4):

        @pl.when(jnp.logical_not(exists(o)))
        def _():
            near[:, o] = jnp.zeros((groups, 2, rows, HEAD), near.dtype)

    @pl.when(jnp.logical_not(has_behind))
    def _():
        for g in range(groups):
            for part in range(2):
                if 2 * g + part in GRAD_DIRECT:
                    grecv[g, 4, part] = jnp.zeros((rows, HEAD), grecv.dtype)

    for g in range(groups):
        kv_load(g, 0).wait()
        kv_load(g, 1).wait()
    pl.semaphore_wait(barrier, 2 + has_ahead.astype(jnp.int32) + has_behind.astype(jnp.int32))

    for g in range(groups):
        for part in range(2):
            partner_copy(g, part).start()
        for part in range(2):
            beside_copy(g, part).start()

    own_block = slot_ref[me]
    live_count = count_ref[own_block]
    chosen = []
    bias = []
    for j in (1, 2):
        wanted = blocks_ref[j, own_block]
        hits = []
        for o in range(4):
            there = jnp.clip(me + OFFSETS[o], 0, n - 1)
            hits.append(exists(o) & (slot_ref[there] == wanted) & (live_count > j))
        chosen.append(hits)
        bias.append(jnp.where(hits[0] | hits[1] | hits[2] | hits[3], 0.0, NEG).astype(jnp.float32))

    def pick(g, part, hits):
        value = near[g, 0, part]
        for o in range(1, 4):
            value = jnp.where(hits[o], near[g, o, part], value)
        return value

    def from_diag(g):
        @pl.when(has_behind)
        def _():
            for part in range(2):
                near_wait(g, part, diag_slot)

                @pl.when(jnp.logical_not(from_partner))
                def _():
                    relay_copy(g, part).start()

    def plus(g, part, slot, place):
        both = gsend[g, slot, part].astype(jnp.float32) + grecv[g, place, part].astype(jnp.float32)
        gsend[g, slot, part] = both.astype(jnp.bfloat16)

    def combine(g):
        for part in range(2):

            @pl.when(has_forward)
            def _():
                passed_grad(g, part).wait_recv()
                plus(g, part, forward, 1)

            send_diag(g, part, jnp.logical_not(from_partner))
            send_partner(g, part, from_partner)

    def send_diag(g, part, mine):
        mine = jnp.logical_and(mine, has_behind)
        direct = among(2 * g + part, GRAD_DIRECT)

        @pl.when(jnp.logical_and(mine, direct))
        def _():
            diag_grad(g, part).start()

        @pl.when(jnp.logical_and(mine, jnp.logical_not(direct)))
        def _():
            behind_grad(g, part).start()

    def send_partner(g, part, mine):
        direct = among(2 * g + part, GRAD_DIRECT)

        @pl.when(jnp.logical_and(mine, jnp.logical_or(direct, jnp.logical_not(has_ahead))))
        def _():
            partner_grad(g, part).start()

    def add_ahead(g):
        for part in range(2):

            @pl.when(jnp.logical_and(has_ahead, jnp.logical_not(among(2 * g + part, GRAD_DIRECT))))
            def _():
                grad_copy(g, part, 0, 2, 0, sibling).wait_recv()
                plus(g, part, partner_slot, 2)
                partner_grad(g, part).start()

    def at(index, pred, action):
        pl.when(pred)(functools.partial(action, index))

    others = pl.ds(rows, 2 * rows)

    def stacked(source, g, pair):
        starts = [pl.multiple_of(g * wide + (2 * pair + i) * HEAD, HEAD) for i in range(2)]
        return jnp.concatenate([source[:, pl.ds(s, HEAD)] for s in starts], axis=0)

    def weigh(g, pair, first, shifts):
        total = jnp.zeros((8, 2 * rows), jnp.float32)
        dot = jnp.zeros((8, 2 * rows), jnp.float32)
        height = rows // 2
        for j, shift in enumerate(shifts):
            for c in range(0, height, CHUNK):
                at_rows = pl.ds(first + j * height + c, CHUNK)
                weight = jnp.exp2(score[g, pair, at_rows] * (scale * LOG2E) - shift)
                score[g, pair, at_rows] = weight
                total = total + jnp.sum(weight.reshape(CHUNK // 8, 8, 2 * rows), axis=0)
                both = weight * pgrad[g, pair, at_rows]
                dot = dot + jnp.sum(both.reshape(CHUNK // 8, 8, 2 * rows), axis=0)
        return jnp.sum(total, axis=0, keepdims=True), jnp.sum(dot, axis=0, keepdims=True)

    def normalised(g, pair, part, factor):
        prob = score[g, pair, part] * stats[g, pair, factor : factor + 1]
        score_grads = prob * (pgrad[g, pair, part] - stats[g, pair, 5:6])
        return prob.astype(jnp.bfloat16), score_grads.astype(jnp.bfloat16)

    def products(g, pair, rounded, score_grads, key_grad, value_grad):
        return (
            key_grad + jnp.dot(score_grads, stacked(q, g, pair), preferred_element_type=jnp.float32),
            value_grad + jnp.dot(rounded, stacked(do, g, pair), preferred_element_type=jnp.float32),
        )

    def own_part(g, carry):
        for copy in load_copies(g):
            copy.wait()
        keys = kv[g, 0]
        values = kv[g, 1]
        for pair in range(pairs):
            raw = lax.dot_general(keys, stacked(q, g, pair), NT, preferred_element_type=jnp.float32)
            best = jnp.max(raw, axis=0, keepdims=True) * (scale * LOG2E)
            score[g, pair, pl.ds(0, rows)] = raw
            pgrad[g, pair, pl.ds(0, rows)] = lax.dot_general(
                values, stacked(do, g, pair), NT, preferred_element_type=jnp.float32
            )
            total, dot = weigh(g, pair, 0, [best] * 2)
            stats[g, pair, 0:1] = best
            stats[g, pair, 1:2] = total
            stats[g, pair, 2:3] = dot
        return carry

    def step(g, carry):
        for part in range(2):
            near_wait(g, part, beside)

        @pl.when(has_passed)
        def _():
            for part in range(2):
                near_wait(g, part, passed)

        for part in range(2):
            for j in range(2):
                picked[g, part, pl.ds(j * rows, rows)] = pick(g, part, chosen[j])
        keys = picked[g, 0]
        values = picked[g, 1]

        def matmuls(pair):
            raw = lax.dot_general(keys, stacked(q, g, pair), NT, preferred_element_type=jnp.float32)
            best = stats[g, pair, 0:1]
            for j in range(2):
                top = jnp.max(raw[j * rows : (j + 1) * rows], axis=0, keepdims=True) * (scale * LOG2E)
                best = jnp.maximum(best, top + bias[j])
            score[g, pair, others] = raw
            pgrad[g, pair, others] = lax.dot_general(
                values, stacked(do, g, pair), NT, preferred_element_type=jnp.float32
            )
            return best

        def softmax(pair, best):
            factor = jnp.exp2(stats[g, pair, 0:1] - best)
            shifts = [best - bias[j // 2] for j in range(4)]
            total, dot = weigh(g, pair, rows, shifts)
            inverse = 1.0 / (total + stats[g, pair, 1:2] * factor)
            delta = (dot + stats[g, pair, 2:3] * factor) * inverse
            stats[g, pair, 3:4] = inverse * factor
            stats[g, pair, 4:5] = inverse
            stats[g, pair, 5:6] = delta

        def sums(pair, key_grad, value_grad):
            return products(g, pair, *normalised(g, pair, others, 4), key_grad, value_grad)

        key_grad = jnp.zeros((2 * rows, HEAD), jnp.float32)
        value_grad = jnp.zeros((2 * rows, HEAD), jnp.float32)
        best0 = matmuls(0)
        best1 = matmuls(1)
        softmax(0, best0)
        best2 = matmuls(2)
        key_grad, value_grad = sums(0, key_grad, value_grad)
        softmax(1, best1)
        at(g - 1, g > 0, combine)
        at(g + 1, g + 1 < groups, from_diag)
        best3 = matmuls(3)
        key_grad, value_grad = sums(1, key_grad, value_grad)
        softmax(2, best2)
        key_grad, value_grad = sums(2, key_grad, value_grad)
        softmax(3, best3)
        key_grad, value_grad = sums(3, key_grad, value_grad)
        for part, grad in ((0, key_grad * scale), (1, value_grad)):
            first = grad[:rows].astype(jnp.bfloat16)
            second = grad[rows:].astype(jnp.bfloat16)
            nothing = jnp.zeros_like(first)
            for o in range(4):
                gsend[g, o, part] = jnp.where(chosen[0][o], first, jnp.where(chosen[1][o], second, nothing))

        for part in range(2):

            @pl.when(has_passed)
            def _():
                passed_grad(g, part).start()

            send_diag(g, part, from_partner)
            send_partner(g, part, jnp.logical_not(from_partner))
        for part in range(2):
            beside_grad(g, part).start()
        return carry

    def results(g, carry):
        keys_t = jnp.concatenate([kv[g, 0], picked[g, 0]], axis=0).T
        values_t = jnp.concatenate([kv[g, 1], picked[g, 1]], axis=0).T
        key_grad = jnp.zeros((rows, HEAD), jnp.float32)
        value_grad = jnp.zeros((rows, HEAD), jnp.float32)
        for pair in range(pairs):
            own_rounded, own_grads = normalised(g, pair, pl.ds(0, rows), 3)
            rounded, score_grads = normalised(g, pair, others, 4)
            key_grad, value_grad = products(g, pair, own_rounded, own_grads, key_grad, value_grad)
            rounded = jnp.concatenate([own_rounded, rounded], axis=0)
            score_grads = jnp.concatenate([own_grads, score_grads], axis=0)
            mixed = jnp.dot(values_t, rounded, preferred_element_type=jnp.float32)
            query_grad = jnp.dot(keys_t, score_grads, preferred_element_type=jnp.float32) * scale
            mixed = mixed.astype(jnp.bfloat16).T
            query_grad = query_grad.astype(jnp.bfloat16).T
            for i in range(2):
                where = pl.ds(pl.multiple_of(g * wide + (2 * pair + i) * HEAD, HEAD), HEAD)
                att[:, where] = mixed[i * rows : (i + 1) * rows]
                dq[:, where] = query_grad[i * rows : (i + 1) * rows]
        own_grad[g, 0] = key_grad * scale
        own_grad[g, 1] = value_grad
        at(groups - 1, g == 0, combine)
        at(g + 1, g + 2 < groups, add_ahead)
        return carry

    lax.fori_loop(0, groups, own_part, 0)

    for g in range(groups):
        for part in range(2):
            near_wait(g, part, partner_slot)
            if g not in KV_DIRECT:

                @pl.when(has_ahead)
                def _():
                    ahead_copy(g, part).start()

            @pl.when(from_partner)
            def _():
                relay_copy(g, part).start()

        if g == 0:

            @pl.when(has_behind)
            def _():
                for h in KV_DIRECT:
                    for part in range(2):
                        diag_copy(h, part).start()

    from_diag(0)
    lax.fori_loop(0, groups, step, 0)
    add_ahead(0)
    lax.fori_loop(0, groups, results, 0)
    def finish(g, carry):
        for part in range(2):
            direct = among(2 * g + part, GRAD_DIRECT)
            beside_grad(g, part).wait_recv()
            total = own_grad[g, part] + grecv[g, 0, part].astype(jnp.float32)
            where = pl.ds(pl.multiple_of(part * kv_width + g * HEAD, HEAD), HEAD)

            @pl.when(jnp.logical_and(direct, has_behind))
            def _():
                grad_copy(g, part, 0, 4, 0, partner).wait_recv()

            grad_copy(g, part, 0, 3, 0, partner).wait_recv()
            total = total + grecv[g, 3, part].astype(jnp.float32)

            @pl.when(direct)
            def _():
                kvg[:, where] = (total + grecv[g, 4, part].astype(jnp.float32)).astype(jnp.bfloat16)

            @pl.when(jnp.logical_not(direct))
            def _():
                kvg[:, where] = total.astype(jnp.bfloat16)

        return carry

    def drain_near(g, carry):
        direct = among(g, KV_DIRECT)
        for part in range(2):
            partner_copy(g, part).wait_send()
            beside_copy(g, part).wait_send()

            @pl.when(jnp.logical_and(direct, has_behind))
            def _():
                diag_copy(g, part).wait_send()

            @pl.when(jnp.logical_and(jnp.logical_not(direct), has_ahead))
            def _():
                ahead_copy(g, part).wait_send()

            @pl.when(has_forward)
            def _():
                relay_copy(g, part).wait_send()

        return carry

    def drain_grads(g, carry):
        for part in range(2):
            beside_grad(g, part).wait_send()
            partner_grad(g, part).wait_send()

            @pl.when(has_passed)
            def _():
                passed_grad(g, part).wait_send()

            @pl.when(has_behind)
            def _():
                behind_grad(g, part).wait_send()

        return carry

    add_ahead(groups - 1)
    lax.fori_loop(0, groups, drain_near, 0)
    lax.fori_loop(0, groups, finish, 0)
    lax.fori_loop(0, groups, drain_grads, 0)


def flush(att, dq, kvg, att_out, dq_out, kvg_out, out_sem):
    width = kvg.shape[1]
    pieces = [(kvg, kvg_out, 0)]
    for start in range(0, att.shape[1], width):
        pieces.append((att, att_out, start))
        pieces.append((dq, dq_out, start))
    stores = []
    for i, (source, result, start) in enumerate(pieces):
        part = pl.ds(start, width)
        stores.append(pltpu.make_async_copy(source.at[:, part], result.at[:, part], out_sem.at[i]))
    for store in stores:
        store.start()
    for store in stores:
        store.wait()


def body(queries, keys_values, out_grad, key_blocks, key_count, block_at_slot):
    n = lax.axis_size("ctx")
    rows, width = queries.shape
    kv_width = keys_values.shape[1] // 2
    groups = kv_width // HEAD
    repeats = width // kv_width
    scalars = pl.BlockSpec(memory_space=pltpu.SMEM)
    wide = pltpu.VMEM((rows, width), jnp.bfloat16)
    narrow = pltpu.VMEM((rows, 2 * kv_width), jnp.bfloat16)
    dma = pltpu.SemaphoreType.DMA
    shapes = (
        jax.ShapeDtypeStruct((rows, width), jnp.bfloat16),
        jax.ShapeDtypeStruct((rows, width), jnp.bfloat16),
        jax.ShapeDtypeStruct((rows, 2 * kv_width), jnp.bfloat16),
    )

    def blocks(*lead, dtype=jnp.bfloat16):
        return pltpu.VMEM((*lead, rows, HEAD), dtype)

    pieces = 2 * (width // (2 * kv_width)) + 1
    held = pl.BlockSpec(memory_space=pltpu.VMEM)
    pair_float = pltpu.VMEM((groups, repeats // 2, 3 * rows, 2 * rows), jnp.float32)
    pair_stats = pltpu.VMEM((groups, repeats // 2, 8, 2 * rows), jnp.float32)
    results = pl.pallas_call(
        functools.partial(kernel, n, groups, repeats),
        out_shape=(wide, wide, narrow),
        in_specs=[scalars] * 3 + [pl.BlockSpec(memory_space=pltpu.HBM)] * 3,
        out_specs=(held, held, held),
        scratch_shapes=[
            wide, blocks(groups, 2), wide, blocks(groups, 4, 2),
            pltpu.VMEM((groups, 2, 2 * rows, HEAD), jnp.bfloat16), pair_float, pair_float, pair_stats,
            blocks(groups, 2, dtype=jnp.float32), blocks(groups, 4, 2), blocks(groups, 5, 2),
            dma((groups, 2)), dma((groups, 2)),
            dma((groups, 4, 2)), dma((groups, 4, 2)), dma((groups, 4, 2)), dma((groups, 5, 2)),
        ],
        compiler_params=pltpu.CompilerParams(
            collective_id=0, has_side_effects=True, vmem_limit_bytes=61 * 1024 * 1024
        ),
    )(key_blocks.T, key_count, block_at_slot, queries, keys_values, out_grad)
    return pl.pallas_call(
        flush,
        out_shape=shapes,
        in_specs=[held] * 3,
        out_specs=(pl.BlockSpec(memory_space=pltpu.HBM),) * 3,
        scratch_shapes=[dma((pieces,))],
        compiler_params=pltpu.CompilerParams(vmem_limit_bytes=16 * 1024 * 1024),
    )(*results)


def solution(mesh):
    sharded = P(("groups", "ctx"), None)
    return jax.shard_map(
        body,
        mesh=mesh,
        in_specs=(sharded, sharded, sharded, P("groups", None), P("groups"), P("groups")),
        out_specs=(sharded, sharded, sharded),
        check_vma=False,
    )
```
